32 devices in a mesh: ctx: 32 (over z, y, x, core).
Axes of the slice: x: 2, y: 2, z: 4, core: 2. Of those that a mesh axis runs over, the one named last changes fastest.
Arguments:
- queries: bfloat16 [32768, 2048], P('ctx'), may hold values from -6 to 6
- keys: bfloat16 [32768, 2048], P('ctx'), may hold values from -6 to 6
- values: bfloat16 [32768, 2048], P('ctx'), may hold values from -6 to 6
- level_gate: bfloat16 [32768, 128], P('ctx'), may hold values from 0.19921875 to 2
- norm_gain: float32 [2048], replicated, may hold values from 0.5 to 1.5
- out_weight: bfloat16 [2048, 2048], P('ctx'), may hold values from -0.125 to 0.125
Outputs:
- layer_out: bfloat16 [32768, 2048], P('ctx')
The draws below stay inside these ranges and needn't reach their ends.
All inputs are finite; a program needn't handle non-finite values.
Results may differ from the reference program's by a relative error of at most 0.0057.
Values may be sent and summed in bfloat16 or wider, within the bound.
A program may use at most 192 MiB of HBM per device.

```python
import math
import jax
import jax.numpy as jnp
from jax import lax

HEADS = 16
HEAD = 128
D = 2048
TOK_DEV = 1024
GATES = 8
TOKENS = 32768
N_CTX = 32


def block_levels(rng, dims, split, smallest, top_value):
    def one(dim, blocks):
        draws = jax.random.uniform(jax.random.fold_in(jax.random.fold_in(rng, 6), dim), (blocks,), jnp.float32, smallest / len(split), top_value / len(split))
        return jnp.repeat(jnp.exp(draws), dims[dim] // blocks).reshape((-1,) + (1,) * (len(dims) - dim - 1))

    loudness = one(*split[0])
    for cut in split[1:]:
        loudness = loudness * one(*cut)
    return loudness


def normal_values(key, dims, width, most, split=(), held_as=jnp.bfloat16):
    result = width * jax.random.normal(key, dims, jnp.float32)
    if split:
        result = result * block_levels(key, dims, split, -0.22, 0.18)
    return jnp.clip(result, -most, most).astype(held_as)


def setup_inputs(seed: int = 0) -> dict:
    seeds = jax.random.split(jax.random.key(seed), 7)
    queries = normal_values(seeds[0], (TOKENS, D), 1.0, 6.0, ((0, 32),))
    keys = normal_values(seeds[1], (TOKENS, D), 1.0, 6.0, ((0, 32),))
    values = normal_values(seeds[2], (TOKENS, D), 1.0, 6.0, ((0, 32),))
    level_gate = jnp.clip(jnp.exp(math.log(2.0) - 2.306499 * jax.random.uniform(seeds[3], (TOKENS, GATES * HEADS), jnp.float32) ** block_levels(seeds[3], (TOKENS, GATES * HEADS), ((0, 32),), -0.2, 0.2)), 0.19921875, 2.0).astype(jnp.bfloat16)
    norm_gain = jnp.clip(1.0 + 0.1 * jax.random.normal(seeds[4], (D,), jnp.float32), 0.5, 1.5)
    out_weight = normal_values(seeds[5], (D, D), D ** -0.5, 0.125, ((0, 32),))
    return dict(queries=queries, keys=keys, values=values, level_gate=level_gate, norm_gain=norm_gain, out_weight=out_weight)


EPSILON = 1e-06
HIGH = lax.Precision.HIGHEST

def within_shard(query_heads, key_heads, value_heads, level_weights):
    scores = jnp.einsum('thd,shd->hts', query_heads.astype(jnp.float32), key_heads.astype(jnp.float32), precision=HIGH)
    positions = jnp.arange(query_heads.shape[0], dtype=jnp.int32)
    causal = positions[:, None] >= positions[None, :]
    weighted = jnp.where(causal[None], scores, jnp.float32(0.0)).astype(jnp.bfloat16)
    mixed = jnp.einsum('hts,shd->thd', weighted.astype(jnp.float32), value_heads.astype(jnp.float32), precision=HIGH)
    return mixed * level_weights[:, 0, :, None]

def finish(summed, norm_gain):
    squares = lax.optimization_barrier(jnp.mean(summed * summed, axis=-1, keepdims=True))
    normed = summed * lax.rsqrt(squares + EPSILON) * norm_gain.reshape(HEADS, HEAD)
    return normed.reshape(summed.shape[0], HEADS * HEAD).astype(jnp.bfloat16)

def reference(queries, keys, values, level_gate, norm_gain, out_weight):
    shards = N_CTX
    levels = shards.bit_length() - 1
    query_all = queries.reshape(shards, TOK_DEV, HEADS, HEAD)
    key_all = keys.reshape(shards, TOK_DEV, HEADS, HEAD)
    value_all = values.reshape(shards, TOK_DEV, HEADS, HEAD)
    weight_all = level_gate.reshape(shards, TOK_DEV, GATES, HEADS).astype(jnp.float32)

    def shard_state(pair):
        return jnp.einsum('shd,she->hde', pair[0].astype(jnp.float32), pair[1].astype(jnp.float32), precision=HIGH)
    states = lax.map(shard_state, (key_all, value_all))
    tables = [states.reshape(shards >> level_index, 1 << level_index, HEADS, HEAD, HEAD).sum(1) for level_index in range(levels)]

    def one_shard(position):
        query_heads = query_all[position]
        level_weights = weight_all[position]
        summed = within_shard(query_heads, key_all[position], value_all[position], level_weights)
        for level_index in range(levels):
            upper_half = position >> level_index & 1 == 1
            block = jnp.maximum((position >> level_index) - 1, 0)
            bucket = jnp.where(upper_half, tables[level_index][block], jnp.float32(0.0)).astype(jnp.bfloat16)
            product = jnp.einsum('thd,hde->the', query_heads.astype(jnp.float32), bucket.astype(jnp.float32), precision=HIGH)
            summed = summed + level_weights[:, level_index + 1, :, None] * product
        return finish(summed, norm_gain)
    mixed = lax.map(one_shard, jnp.arange(shards, dtype=jnp.int32))
    mixed = mixed.reshape(shards * TOK_DEV, HEADS * HEAD)
    return jnp.dot(mixed, out_weight, preferred_element_type=jnp.float32).astype(jnp.bfloat16)
```

```python
import functools
import jax
import jax.numpy as jnp
from jax import lax
from jax.experimental import pallas as pl
from jax.experimental.pallas import tpu as pltpu
from jax.sharding import PartitionSpec as P

HEAD = 128
CHUNK = 256
GROUPS = 4
EPSILON = 1e-06
F32 = jnp.float32
BF16 = jnp.bfloat16
MESH = pl.DeviceIdType.MESH


def dot(a, b, dims=((1,), (0,))):
    return lax.dot_general(a, b, (dims, ((), ())), preferred_element_type=F32)


def other(me, mask):
    bit = 1
    out = me
    while bit <= mask:
        if mask & bit:
            out = out + bit * (1 - 2 * ((me // bit) % 2))
        bit *= 2
    return out


def transfers(levels, columns):
    names = [("first", i) for i in range(2)]
    for l in range(1, levels):
        names += [(kind, l, g) for kind in ("stage", "pass") for g in range(GROUPS)]
    names += [("z", j, s) for j in range(1, columns) for s in range(2)]
    names += [(kind, j, s) for kind in ("x", "y") for j in range(columns) for s in range(2)]
    names += [(kind, j) for kind in ("dx", "dy") for j in range(columns) if j != 1]
    names += [("dz", s) for s in range(2)]
    names += [(kind, j) for kind in ("c0", "c2", "c4", "c6") for j in range(columns)]
    return {name: at for at, name in enumerate(names)}


def plane_rows(me, column, part):
    first_row = other(me, column << 3) // 8 * (8 * part)
    return pl.ds(pl.multiple_of(first_row, 8 * part), 8 * part)


def splits(part):
    return 4 * part % HEAD == 0


def half_plane_rows(me, mask, part):
    first_row = other(me, mask) // 4 * (4 * part)
    return pl.ds(pl.multiple_of(first_row, 4 * part), 4 * part)


def kernel(n, q_hbm, k_hbm, v_hbm, gate_ref, gain_ref, w_ref, acc, k, whole,
           q, v, turned, gates, gains, prefix, total, running, buckets, first, sends,
           load_sem, send_sem, recv_sem):
    rows, width = q.shape
    heads, chunks = width // HEAD, rows // CHUNK
    half = heads // 2
    group = half // GROUPS
    levels = n.bit_length() - 1
    columns = n // 8
    top = levels - 1
    part = w_ref.shape[0]
    ids = transfers(levels, columns)
    me = lax.axis_index("ctx")
    core = me % 2
    column = me // 8
    flags = [(me // (1 << l)) % 2 for l in range(levels)]

    def part_of(core_bit, g):
        return pl.ds(core_bit * half + g * group, group)

    def column_range(side):
        return pl.ds(pl.multiple_of(side * half * HEAD, half * HEAD), half * HEAD)

    def load(hbm, buffer, kind, i, c):
        at = pl.ds(c * CHUNK, CHUNK)
        sem = load_sem.at[kind, i * chunks + c]
        if kind == 2:
            return pltpu.make_async_copy(hbm.at[at], buffer.at[at], sem)
        cols = column_range(1 - core if i == 0 else core)
        return pltpu.make_async_copy(hbm.at[at, cols], buffer.at[at, cols], sem)

    for i in range(2):
        for c in range(chunks):
            load(k_hbm, k, 0, i, c).start()
            load(v_hbm, v, 1, i, c).start()
    for c in range(chunks):
        load(q_hbm, q, 2, 0, c).start()

    masks = sorted({1, 2, 4} | {j << 3 for j in range(1, columns)})
    barrier = pltpu.get_barrier_semaphore()
    for mask in masks:
        pl.semaphore_signal(barrier, inc=1, device_id=(other(me, mask),), device_id_type=MESH)
    pl.semaphore_wait(barrier, len(masks))

    def copy(name, src, dst, device):
        at = ids[name]
        return pltpu.make_async_remote_copy(
            src_ref=src, dst_ref=dst, send_sem=send_sem.at[at], recv_sem=recv_sem.at[at],
            device_id=(device,), device_id_type=MESH,
        )

    side_width = whole.shape[1] // 2

    def shard(mask, side=None):
        at = pl.ds(pl.multiple_of(other(me, mask) * part, part), part)
        if side is None:
            return whole.at[at]
        return whole.at[at, pl.ds(side * side_width, side_width)]

    def own(side):
        return w_ref.at[:, pl.ds(side * side_width, side_width)]

    def place(l):
        return column % (2 << (l - 3))

    def receives(l):
        return flags[l] == 1

    def origin(l):
        return place(l) == (1 << (l - 3)) - 1

    def relays(l):
        return jnp.logical_and(place(l) >= 1 << (l - 3), place(l) < (2 << (l - 3)) - 1)

    def send(name, relay=False):
        kind, j = name[:2]
        if kind == "first":
            at = pl.ds((1 - core if j == 0 else core) * half, half)
            return copy(name, first.at[at], buckets.at[0, at], other(me, 1))
        if kind in ("stage", "pass"):
            g = name[2]
            here = buckets.at[j, part_of(core, g)]
            if kind == "pass":
                return copy(name, here, here, other(me, 1))
            src = here if relay else sends.at[j - 1, pl.ds(g * group, group)]
            return copy(name, src, here, other(me, 1 << j) if j < 3 else me + 8)
        if kind == "dz":
            return copy(name, shard(6, j), shard(6, j), other(me, 8))
        col = j << 3
        if kind == "z":
            low = j & -j
            s = name[2]
            if low == j:
                return copy(name, own(s), shard(0, s), other(me, col))
            at = shard((j ^ low) << 3, s)
            return copy(name, at, at, other(me, low << 3))
        if kind in ("x", "y"):
            s = name[2]
            src = own(s) if j == 0 else shard(col, s)
            return copy(name, src, shard(col, s), other(me, {"x": 2, "y": 4}[kind]))
        if kind == "dy":
            return copy(name, shard(2 ^ col, 0), shard(2 ^ col, 0), other(me, 4))
        if kind == "dx":
            return copy(name, shard(4 ^ col, 1), shard(4 ^ col, 1), other(me, 2))
        mask = int(kind[1]) ^ col
        return copy(name, w_ref if mask == 0 else shard(mask), shard(mask), other(me, 1))

    def arrival(name):
        kind, j = name[:2]
        if kind == "first":
            dst = buckets.at[0, pl.ds((core if j == 0 else 1 - core) * half, half)]
        elif kind == "stage":
            dst = buckets.at[j, part_of(core, name[2])]
        elif kind == "pass":
            dst = buckets.at[j, part_of(1 - core, name[2])]
        elif kind == "dz":
            dst = shard(6 ^ 8, j)
        else:
            col = j << 3
            if kind == "z":
                dst = shard(col, name[2])
            elif kind in ("x", "y"):
                dst = shard({"x": 2, "y": 4}[kind] ^ col, name[2])
            elif kind == "dy":
                dst = shard(6 ^ col, 0)
            elif kind == "dx":
                dst = shard(6 ^ col, 1)
            else:
                dst = shard(1 ^ int(kind[1]) ^ col)
        return copy(name, dst, dst, other(me, 1))

    def start(*name):
        send(name).start()

    def receive(*name):
        arrival(name).wait_recv()

    mine = pltpu.make_async_copy(w_ref, shard(0), load_sem.at[3, 0])
    mine.start()
    for s in range(2):
        start("x", 0, s)
        start("y", 0, 1 - s)
    for l in range(3, levels):
        for s in range(2):
            start("z", 1 << (l - 3), s)
    start("c0", 0)

    for l in range(3, levels):
        @pl.when(flags[l] == 0)
        def _(l=l):
            buckets[l] = jnp.zeros(buckets.shape[1:], BF16)

    for b in range(rows // HEAD):
        at = slice(b * HEAD, (b + 1) * HEAD)
        tile = gate_ref[at, :].astype(F32).T
        scale = [jnp.ones((heads, HEAD), F32)] + [
            jnp.full((heads, HEAD), flags[l].astype(F32)) for l in range(levels)
        ]
        rest = tile.shape[0] - heads * len(scale)
        if rest:
            scale.append(jnp.zeros((rest, HEAD), F32))
        gates[:, at] = tile * jnp.concatenate(scale, axis=0)
    for h in range(heads):
        cols = slice(h * HEAD, (h + 1) * HEAD)
        gains[cols, :] = jnp.broadcast_to(gain_ref[:, cols], (HEAD, HEAD)).T

    total[...] = jnp.zeros_like(total)
    for i in range(2):
        side = 1 - core if i == 0 else core

        def state_step(c, carry):
            load(k_hbm, k, 0, i, c).wait()
            load(v_hbm, v, 1, i, c).wait()
            at = pl.ds(pl.multiple_of(c * CHUNK, CHUNK), CHUNK)
            for e in range(half):
                h = side * half + e
                cols = pl.ds(pl.multiple_of(h * HEAD, HEAD), HEAD)
                before = total[h]
                prefix[c, h] = before.astype(BF16)
                flipped = v[at, cols].T
                turned[cols, at] = flipped
                total[h] = before + dot(flipped, k[at, cols])
            return carry

        lax.fori_loop(0, chunks, state_step, 0)
        at = pl.ds(side * half, half)
        first[at] = total[at].astype(BF16)
        start("first", i)

    def send_on(l, g):
        at = pl.ds(g * group, group)

        def go():
            sends[l, at] = running[at].astype(BF16)
            start("stage", l + 1, g)

        if l + 1 < 3:
            go()
        else:
            pl.when(origin(l + 1))(go)

    def advance_first():
        receive("first", 0)
        at = pl.ds(core * half, half)
        running[...] = total[at] + buckets[0, at].astype(F32)
        for g in range(GROUPS):
            send_on(0, g)

    def advance(l, g):
        def arrived():
            receive("stage", l, g)
            if l >= 3:
                @pl.when(relays(l))
                def _():
                    send(("stage", l, g), relay=True).start()
            if l + 1 < levels:
                at = pl.ds(g * group, group)
                running[at] = running[at] + buckets[l, part_of(core, g)].astype(F32)

        def passing():
            start("pass", l, g)

        if l < 3:
            arrived()
        else:
            pl.when(receives(l))(arrived)
        if l + 1 < levels:
            send_on(l, g)
        if l < 3:
            passing()
        else:
            pl.when(receives(l))(passing)

    def passed(l, g):
        if l < 3:
            receive("pass", l, g)
        else:
            pl.when(receives(l))(lambda: receive("pass", l, g))

    def z_arrived(j, s):
        receive("z", j, s)

    def z_relay(j, s):
        bit = 1
        while bit < (j & -j):
            start("z", j | bit, s)
            bit *= 2

    def sides_arrived(j):
        for s in range(2):
            receive("x", j, s)
            receive("y", j, s)
        start("c2", j)
        start("c4", j)

    def diagonals(j):
        start("dy", j)
        start("dx", j)

    def diagonal_arrived(j):
        if j == 1:
            for s in range(2):
                receive("dz", s)
        else:
            receive("dy", j)
            receive("dx", j)
        start("c6", j)

    def heads_of(g):
        return [side * half + g * group + e for side in range(2) for e in range(group)]

    def body(function, g, tasks):
        def step(c, carry):
            at = pl.ds(pl.multiple_of(c * CHUNK, CHUNK), CHUNK)
            function(g, c, at)
            for point, task in tasks.items():
                pl.when(c == point)(task)
            return carry

        lax.fori_loop(0, chunks, step, 0)

    def weight(l, h, at):
        row = (l + 1) * heads + h
        return gates[row : row + 1, at]

    def spot(h, c):
        down, across = divmod(h * chunks, heads // 2)
        return slice(down * HEAD, (down + 1) * HEAD), pl.ds(
            pl.multiple_of((across + c) * CHUNK, CHUNK), CHUNK
        )

    def local(g, c, at):
        causal = lax.broadcasted_iota(jnp.int32, (CHUNK, CHUNK), 0) <= lax.broadcasted_iota(
            jnp.int32, (CHUNK, CHUNK), 1
        )
        for h in heads_of(g):
            cols = slice(h * HEAD, (h + 1) * HEAD)
            stack = jnp.concatenate([k[at, cols], prefix[c, h], buckets[0, h]], axis=0)
            product = dot(stack, q[at, cols], ((1,), (1,)))
            scores = jnp.where(causal, product[:CHUNK], 0.0).astype(BF16)
            mixed = dot(turned[cols, at], scores) + product[CHUNK : CHUNK + HEAD]
            acc[spot(h, c)] = mixed * weight(-1, h, at) + product[CHUNK + HEAD :] * weight(0, h, at)

    def add_levels(c, at, h, wanted):
        cols = slice(h * HEAD, (h + 1) * HEAD)
        stack = jnp.concatenate([buckets[l, h] for l in wanted], axis=0)
        product = dot(stack, q[at, cols], ((1,), (1,)))
        sofar = acc[spot(h, c)]
        for i, l in enumerate(wanted):
            sofar = sofar + weight(l, h, at) * product[i * HEAD : (i + 1) * HEAD]
        return sofar

    def middle(g, c, at):
        for h in heads_of(g):
            acc[spot(h, c)] = add_levels(c, at, h, range(1, top - 1))

    def last(g, c, at):
        for h in heads_of(g):
            cols = slice(h * HEAD, (h + 1) * HEAD)
            attended = add_levels(c, at, h, range(top - 1, levels))
            squares = jnp.mean(attended * attended, axis=0, keepdims=True)
            gain = jnp.concatenate([gains[cols, :]] * (CHUNK // HEAD), axis=1)
            normed = attended * lax.rsqrt(squares + EPSILON) * gain
            k[at, cols] = normed.astype(BF16).T

    def task_z1_0():
        z_arrived(1, 0)
        start("y", 1, 0)
        start("x", 1, 0)

    def task_z1_1():
        z_arrived(1, 1)
        start("x", 1, 1)
        start("c0", 1)
        sides_arrived(0)

    advance_first()
    receive("first", 1)
    for c in range(chunks):
        load(q_hbm, q, 2, 0, c).wait()
    body(local, 0, {})
    body(local, 1, {0: task_z1_0})
    body(local, 2, {1: task_z1_1, 3: lambda: advance(1, 0)})
    body(local, 3, {1: lambda: advance(1, 1), 3: lambda: advance(1, 2)})

    def z2_arrived(s):
        z_arrived(2, s)
        start("x", 2, s)

    advance(2, 0)
    advance(1, 3)
    start("y", 1, 1)
    z2_arrived(0)
    advance(2, 1)

    relay_late = relays(top)

    def z3_start():
        for s in range(2):
            start("z", 3, s)

    def before_middle_2():
        z2_arrived(1)
        start("y", 2, 1)
        start("y", 2, 0)
        start("c0", 2)

    for l in range(3, top - 1):
        for g in range(GROUPS):
            advance(l, g)

    def passed_middle(g):
        for l in range(1, top - 1):
            passed(l, g)

    passed_middle(0)
    body(middle, 0, {})
    passed_middle(1)
    body(middle, 1, {0: lambda: advance(2, 2), 2: before_middle_2})
    passed_middle(2)
    body(middle, 2, {0: lambda: advance(2, 3), 2: lambda: pl.when(jnp.logical_not(relay_late))(z3_start)})
    passed_middle(3)
    body(middle, 3, {})
    diagonals(0)
    for g in range(GROUPS):
        advance(top - 1, g)
    for g in range(2):
        advance(top, g)

    def passed_last(g):
        passed(top - 1, g)
        passed(top, g)

    def task_top_3():
        advance(top, 3)
        pl.when(relay_late)(z3_start)

    def task_sides_2():
        sides_arrived(1)
        sides_arrived(2)
        diagonals(2)

    passed_last(0)
    body(last, 0, {1: lambda: advance(top, 2), 3: task_top_3})
    passed_last(1)
    body(last, 1, {})
    passed_last(2)
    body(last, 2, {2: task_sides_2})
    passed_last(3)
    body(last, 3, {})

    def task_diagonal_0():
        diagonal_arrived(0)
        for s in range(2):
            start("dz", s)

    def task_z3(s):
        z_arrived(3, s)
        start("x", 3, s)
        if s == 1:
            start("y", 3, 1)
            start("y", 3, 0)
            start("c0", 3)

    def rest_columns():
        for j in range(4, columns):
            for s in range(2):
                z_arrived(j, s)
                z_relay(j, s)
                start("x", j, s)
                start("y", j, s)
            start("c0", j)
        for j in range(4, columns):
            sides_arrived(j)
            diagonals(j)
        for j in range(4, columns):
            diagonal_arrived(j)

    def project(pieces, fresh, tasks):
        def step(c, carry):
            at = pl.ds(pl.multiple_of(c * CHUNK, CHUNK), CHUNK)
            product = None
            for planes in pieces:
                more = dot(k[at, planes], whole[planes, :])
                product = more if product is None else product + more
            acc[at, :] = product if fresh else acc[at, :] + product
            for point, task in tasks.items():
                pl.when(c == point)(task)
            return carry

        lax.fori_loop(0, chunks, step, 0)

    mine.wait()
    task_diagonal_0()
    for kind in ("c0", "c2", "c4", "c6"):
        receive(kind, 0)
    for kind in ("c0", "c2"):
        receive(kind, 1)
    project(
        [plane_rows(me, 0, part)] + ([half_plane_rows(me, 8, part)] if splits(part) else []), True,
        {0: lambda: task_z3(0), 2: lambda: task_z3(1)},
    )
    diagonal_arrived(2)
    if columns > 4:
        rest_columns()
    for j in range(2, columns):
        if j == 3:
            continue
        for kind in ("c0", "c2", "c4", "c6"):
            receive(kind, j)

        def task_sides_3():
            sides_arrived(3)
            diagonals(3)

        project([plane_rows(me, j, part)], False, {2: task_sides_3} if j == 2 else {})
    for kind in ("c0", "c2"):
        receive(kind, 3)
    if splits(part):
        project([half_plane_rows(me, 24, part)], False, {1: lambda: diagonal_arrived(1)})
    else:
        diagonal_arrived(1)
    diagonal_arrived(3)
    for j in (1, 3):
        for kind in ("c4", "c6"):
            receive(kind, j)
    for name in ids:
        if name[0] == "stage" and name[1] >= 3:
            cond = jnp.logical_or(origin(name[1]), relays(name[1]))
        elif name[0] == "pass" and name[1] >= 3:
            cond = receives(name[1])
        else:
            send(name).wait_send()
            continue
        pl.when(cond)(lambda name=name: send(name).wait_send())


def project_kernel(n, part, acc_ref, normed_ref, whole_ref, out_ref):
    at = pl.ds(pl.multiple_of(pl.program_id(0) * CHUNK, CHUNK), CHUNK)
    me = lax.axis_index("ctx")
    product = acc_ref[at, :]
    for j in (1, 3):
        planes = half_plane_rows(me, (j << 3) ^ 4, part) if splits(part) else plane_rows(me, j, part)
        product = product + dot(normed_ref[at, planes], whole_ref[planes, :])
    out_ref[...] = product.astype(BF16)


def shards(queries, keys, values, level_gate, norm_gain, out_weight):
    n = lax.axis_size("ctx")
    rows, width = queries.shape
    heads, chunks = width // HEAD, rows // CHUNK
    levels = n.bit_length() - 1
    count = len(transfers(levels, n // 8))
    vmem = pl.BlockSpec(memory_space=pltpu.VMEM)
    hbm = pl.BlockSpec(memory_space=pltpu.HBM)
    out_width = out_weight.shape[1]
    weight_rows = n * out_weight.shape[0]
    acc, normed, whole = pl.pallas_call(
        functools.partial(kernel, n),
        out_shape=[
            pltpu.VMEM((rows, width), F32),
            pltpu.VMEM((rows, width), BF16),
            pltpu.VMEM((weight_rows, out_width), BF16),
        ],
        in_specs=[hbm, hbm, hbm, vmem, vmem, vmem],
        out_specs=[vmem] * 3,
        scratch_shapes=[
            pltpu.VMEM((rows, width), BF16),
            pltpu.VMEM((rows, width), BF16),
            pltpu.VMEM((width, rows), BF16),
            pltpu.VMEM((level_gate.shape[1], rows), F32),
            pltpu.VMEM((width, HEAD), F32),
            pltpu.VMEM((chunks, heads, HEAD, HEAD), BF16),
            pltpu.VMEM((heads, HEAD, HEAD), F32),
            pltpu.VMEM((heads // 2, HEAD, HEAD), F32),
            pltpu.VMEM((levels, heads, HEAD, HEAD), BF16),
            pltpu.VMEM((heads, HEAD, HEAD), BF16),
            pltpu.VMEM((levels - 1, heads // 2, HEAD, HEAD), BF16),
            pltpu.SemaphoreType.DMA((4, 2 * chunks)),
            pltpu.SemaphoreType.DMA((count,)),
            pltpu.SemaphoreType.DMA((count,)),
        ],
        compiler_params=pltpu.CompilerParams(
            collective_id=0, has_side_effects=True, vmem_limit_bytes=40 * 1024 * 1024
        ),
        name="layer",
    )(queries, keys, values, level_gate, norm_gain.reshape(1, -1), out_weight)
    return pl.pallas_call(
        functools.partial(project_kernel, n, out_weight.shape[0]),
        grid=(chunks,),
        out_shape=jax.ShapeDtypeStruct((rows, out_width), BF16),
        in_specs=[vmem] * 3,
        out_specs=pl.BlockSpec((CHUNK, out_width), lambda i: (i, 0)),
        compiler_params=pltpu.CompilerParams(vmem_limit_bytes=12 * 1024 * 1024),
        name="project",
    )(acc, normed, whole)


def solution(mesh):
    placed = (P("ctx", None), P("ctx", None), P("ctx", None), P("ctx", None), P(), P("ctx", None))
    return jax.shard_map(
        shards, mesh=mesh, in_specs=placed, out_specs=P("ctx", None), check_vma=False
    )
```

```python
import functools
import jax
import jax.numpy as jnp
from jax import lax
from jax.experimental import pallas as pl
from jax.experimental.pallas import tpu as pltpu
from jax.sharding import PartitionSpec as P

HEAD = 128
CHUNK = 256
GROUPS = 4
EPSILON = 1e-06
F32 = jnp.float32
BF16 = jnp.bfloat16
MESH = pl.DeviceIdType.MESH


def dot(a, b, dims=((1,), (0,))):
    return lax.dot_general(a, b, (dims, ((), ())), preferred_element_type=F32)


def other(me, mask):
    bit = 1
    out = me
    while bit <= mask:
        if mask & bit:
            out = out + bit * (1 - 2 * ((me // bit) % 2))
        bit *= 2
    return out


def transfers(levels, columns):
    names = [("first", i, g) for i in range(2) for g in range(GROUPS)]
    for l in range(1, levels):
        names += [(kind, l, g) for kind in ("stage", "pass") for g in range(GROUPS)]
    names += [("up", s) for s in range(2)] + [("down", s) for s in range(2)]
    names += [("z", j, s) for j in range(columns) for s in range(2)]
    names += [(kind, j, s) for kind in ("x", "y") for j in range(columns) for s in range(2)]
    names += [(kind, j) for kind in ("dx", "dy") for j in range(columns) if j != 1]
    names += [("dz", s) for s in range(2)]
    names += [(kind, j) for kind in ("c0", "c2", "c4", "c6") for j in range(columns)]
    return {name: at for at, name in enumerate(names)}


def nth_column(me, k, columns):
    column = me // 8
    if k < 2:
        return column + k * (1 - 2 * (column % 2))
    pair, step, pairs = column // 2, k // 2, columns // 2
    upper = pair // (pairs // 2)
    low = pair + upper * (pairs - 1 - 2 * pair)
    inside = (step <= 2 * low).astype(jnp.int32)
    near = low + (step + 1) // 2 * (1 - 2 * (step % 2))
    found = inside * near + (1 - inside) * step
    found = found + upper * (pairs - 1 - 2 * found)
    above = (found > pair).astype(jnp.int32)
    return 2 * found + above * (k % 2) + (1 - above) * (1 - k % 2)


def plane_rows(me, k, columns, part):
    return pl.ds(pl.multiple_of(nth_column(me, k, columns) * (8 * part), 8 * part), 8 * part)


def splits(part):
    return 4 * part % HEAD == 0


def half_plane_rows(me, k, columns, far, part):
    here = me // 4 % 2
    first = nth_column(me, k, columns) * 2 + (1 - here if far else here)
    return pl.ds(pl.multiple_of(first * (4 * part), 4 * part), 4 * part)


def kernel(n, q_hbm, k_hbm, v_hbm, gate_hbm, gain_hbm, w_hbm, acc, k, whole,
           q, v, gate_ref, gain_ref, turned, gates, gains, prefix, running, buckets, first, sends,
           load_sem, send_sem, recv_sem):
    rows, width = q.shape
    heads, chunks = width // HEAD, rows // CHUNK
    half = heads // 2
    group = half // GROUPS
    levels = n.bit_length() - 1
    columns = n // 8
    top = levels - 1
    part = w_hbm.shape[0]
    ids = transfers(levels, columns)
    me = lax.axis_index("ctx")
    core = me % 2
    column = me // 8
    flags = [(me // (1 << l)) % 2 for l in range(levels)]

    def part_of(core_bit, g):
        return pl.ds(core_bit * half + g * group, group)

    def side_of(i):
        return 1 - core if i == 0 else core

    def load(hbm, buffer, kind, at, i, g):
        sem = load_sem.at[kind, at]
        if kind == 2:
            rows_here = pl.ds(at * CHUNK, CHUNK)
            return pltpu.make_async_copy(hbm.at[rows_here], buffer.at[rows_here], sem)
        if kind == 3:
            return pltpu.make_async_copy(hbm, buffer, sem)
        wide = group * HEAD
        cols = pl.ds(pl.multiple_of(side_of(i) * (half * HEAD) + g * wide, wide), wide)
        return pltpu.make_async_copy(hbm.at[:, cols], buffer.at[:, cols], sem)

    def loads(i, g):
        at = g * 2 + i
        return load(k_hbm, k, 0, at, i, g), load(v_hbm, v, 1, at, i, g)

    has_up = column < columns - 1
    has_down = column > 0
    barrier = pltpu.get_barrier_semaphore()

    def greet(device):
        pl.semaphore_signal(barrier, inc=1, device_id=(device,), device_id_type=MESH)

    for mask in (1, 2, 4):
        greet(other(me, mask))
    pl.when(has_up)(lambda: greet(me + 8))
    pl.when(has_down)(lambda: greet(me - 8))

    for g in range(GROUPS):
        for i in range(2):
            for one in loads(i, g):
                one.start()
    gate_load = load(gate_hbm, gate_ref, 3, 1, 0, 0)
    gain_load = load(gain_hbm, gain_ref, 3, 2, 0, 0)
    gate_load.start()
    gain_load.start()
    q_loads = [load(q_hbm, q, 2, c, 0, 0) for c in range(chunks)]
    for one in q_loads:
        one.start()

    inside = has_up.astype(jnp.int32) + has_down.astype(jnp.int32)
    pl.semaphore_wait(barrier, 3 + inside)

    def z_sem(at, s):
        return ids["z", 0, 0] + 2 * at + s

    def copy(name, src, dst, device, landing=None):
        at = ids[name]
        landing = at if landing is None else landing
        return pltpu.make_async_remote_copy(
            src_ref=src, dst_ref=dst, send_sem=send_sem.at[at], recv_sem=recv_sem.at[landing],
            device_id=(device,), device_id_type=MESH,
        )

    side_width = whole.shape[1] // 2

    place_of = [nth_column(me, k, columns) for k in range(columns)]

    def block(device, side=None):
        at = pl.ds(pl.multiple_of(device * part, part), part)
        if side is None:
            return whole.at[at]
        return whole.at[at, pl.ds(side * side_width, side_width)]

    def shard(mask, k, side=None):
        return block(other(me, mask) + (place_of[k] - column) * 8, side)

    def own(side):
        return w_hbm.at[:, pl.ds(side * side_width, side_width)]

    def place(l):
        return column % (2 << (l - 3))

    def receives(l):
        return flags[l] == 1

    def origin(l):
        return place(l) == (1 << (l - 3)) - 1

    def relays(l):
        return jnp.logical_and(place(l) >= 1 << (l - 3), place(l) < (2 << (l - 3)) - 1)

    def send(name, relay=False):
        kind, j = name[:2]
        if kind == "first":
            at = part_of(side_of(j), name[2])
            return copy(name, first.at[at], buckets.at[0, at], other(me, 1))
        if kind in ("stage", "pass"):
            g = name[2]
            here = buckets.at[j, part_of(core, g)]
            if kind == "pass":
                return copy(name, here, here, other(me, 1))
            src = here if relay else sends.at[j - 1, pl.ds(g * group, group)]
            return copy(name, src, here, other(me, 1 << j) if j < 3 else me + 8)
        if kind == "dz":
            return copy(name, shard(6, 0, j), shard(6, 0, j), other(me, 8))
        if kind in ("up", "down"):
            return copy(name, own(j), shard(0, 0, j), me + 8 if kind == "up" else me - 8, z_sem(column, j))
        if kind == "z":
            s = name[2]
            at = shard(0, j, s)
            onward = 1 - 2 * (place_of[j] > column).astype(jnp.int32)
            return copy(name, at, at, me + 8 * onward, z_sem(place_of[j], s))
        if kind in ("x", "y"):
            s = name[2]
            src = own(s) if j == 0 else shard(0, j, s)
            return copy(name, src, shard(0, j, s), other(me, {"x": 2, "y": 4}[kind]))
        if kind == "dy":
            return copy(name, shard(2, j, 0), shard(2, j, 0), other(me, 4))
        if kind == "dx":
            return copy(name, shard(4, j, 1), shard(4, j, 1), other(me, 2))
        mask = int(kind[1])
        src = w_hbm if mask == 0 and j == 0 else shard(mask, j)
        return copy(name, src, shard(mask, j), other(me, 1))

    def arrival(name):
        kind, j = name[:2]
        if kind == "first":
            dst = buckets.at[0, part_of(side_of(1 - j), name[2])]
        elif kind == "stage":
            dst = buckets.at[j, part_of(core, name[2])]
        elif kind == "pass":
            dst = buckets.at[j, part_of(1 - core, name[2])]
        elif kind == "dz":
            dst = shard(6, 1, j)
        elif kind == "z":
            dst = shard(0, j, name[2])
            return copy(name, dst, dst, other(me, 1), z_sem(place_of[j], name[2]))
        elif kind in ("x", "y"):
            dst = shard({"x": 2, "y": 4}[kind], j, name[2])
        elif kind == "dy":
            dst = shard(6, j, 0)
        elif kind == "dx":
            dst = shard(6, j, 1)
        else:
            dst = shard(1 ^ int(kind[1]), j)
        return copy(name, dst, dst, other(me, 1))

    def start(*name):
        send(name).start()

    def receive(*name):
        arrival(name).wait_recv()

    mine = pltpu.make_async_copy(w_hbm, shard(0, 0), load_sem.at[3, 0])
    mine.start()
    start("x", 0, 0)
    start("y", 0, 0)
    pl.when(has_up)(lambda: start("up", 0))
    pl.when(has_down)(lambda: start("down", 0))
    start("y", 0, 1)
    pl.when(has_up)(lambda: start("up", 1))
    pl.when(has_down)(lambda: start("down", 1))
    start("c0", 0)

    for l in range(3, levels):
        @pl.when(flags[l] == 0)
        def _(l=l):
            buckets[l] = jnp.zeros(buckets.shape[1:], BF16)

    def states(i, g):
        for one in loads(i, g):
            one.wait()
        for e in range(group):
            h = side_of(i) * half + g * group + e
            cols = pl.ds(pl.multiple_of(h * HEAD, HEAD), HEAD)
            sofar = jnp.zeros((HEAD, HEAD), F32)
            for c in range(chunks):
                at = slice(c * CHUNK, (c + 1) * CHUNK)
                prefix[c, h] = sofar.astype(BF16)
                flipped = v[at, cols].T
                turned[cols, at] = flipped
                sofar = sofar + dot(flipped, k[at, cols])
            first[h] = sofar.astype(BF16)
            if i == 1:
                running[g * group + e] = sofar
        start("first", i, g)

    def send_on(l, g):
        at = pl.ds(g * group, group)

        def go():
            sends[l, at] = running[at].astype(BF16)
            start("stage", l + 1, g)

        if l + 1 < 3:
            go()
        else:
            pl.when(origin(l + 1))(go)

    def advance_first(g):
        receive("first", 0, g)
        at = pl.ds(g * group, group)
        running[at] = running[at] + buckets[0, part_of(core, g)].astype(F32)
        send_on(0, g)

    def advance(l, g):
        def arrived():
            receive("stage", l, g)
            if l >= 3:
                @pl.when(relays(l))
                def _():
                    send(("stage", l, g), relay=True).start()
            if l + 1 < levels:
                at = pl.ds(g * group, group)
                running[at] = running[at] + buckets[l, part_of(core, g)].astype(F32)

        def passing():
            start("pass", l, g)

        if l < 3:
            arrived()
        else:
            pl.when(receives(l))(arrived)
        if l + 1 < levels:
            send_on(l, g)
        if l < 3:
            passing()
        else:
            pl.when(receives(l))(passing)

    def passed(l, g):
        if l < 3:
            receive("pass", l, g)
        else:
            pl.when(receives(l))(lambda: receive("pass", l, g))

    def forwards(k):
        down = place_of[k] > column
        return jnp.logical_or(jnp.logical_and(down, has_down), jnp.logical_and(jnp.logical_not(down), has_up))

    def z_forward(k, s):
        pl.when(forwards(k))(lambda: start("z", k, s))

    def z_arrived(k, s):
        receive("z", k, s)

    def sides_arrived(j):
        for s in range(2):
            receive("x", j, s)
            receive("y", j, s)
        start("c2", j)
        start("c4", j)

    def diagonals(j):
        start("dy", j)
        start("dx", j)

    def diagonal_arrived(j):
        if j == 1:
            for s in range(2):
                receive("dz", s)
        else:
            receive("dy", j)
            receive("dx", j)
        start("c6", j)

    def heads_of(g):
        return [side * half + g * group + e for side in range(2) for e in range(group)]

    def body(function, g, tasks):
        for c in range(chunks):
            function(g, c, slice(c * CHUNK, (c + 1) * CHUNK))
            if c in tasks:
                tasks[c]()

    def weight(l, h, at):
        row = (l + 1) * heads + h
        return gates[row : row + 1, at]

    def spot(h, c):
        down, across = divmod(h * chunks, heads // 2)
        return slice(down * HEAD, (down + 1) * HEAD), slice((across + c) * CHUNK, (across + c + 1) * CHUNK)

    def local(g, c, at):
        causal = lax.broadcasted_iota(jnp.int32, (CHUNK, CHUNK), 0) <= lax.broadcasted_iota(
            jnp.int32, (CHUNK, CHUNK), 1
        )
        for h in heads_of(g):
            cols = slice(h * HEAD, (h + 1) * HEAD)
            stack = jnp.concatenate([k[at, cols], prefix[c, h], buckets[0, h]], axis=0)
            product = dot(stack, q[at, cols], ((1,), (1,)))
            scores = jnp.where(causal, product[:CHUNK], 0.0).astype(BF16)
            mixed = dot(turned[cols, at], scores) + product[CHUNK : CHUNK + HEAD]
            acc[spot(h, c)] = mixed * weight(-1, h, at) + product[CHUNK + HEAD :] * weight(0, h, at)

    def add_levels(c, at, h, wanted):
        cols = slice(h * HEAD, (h + 1) * HEAD)
        stack = jnp.concatenate([buckets[l, h] for l in wanted], axis=0)
        product = dot(stack, q[at, cols], ((1,), (1,)))
        sofar = acc[spot(h, c)]
        for i, l in enumerate(wanted):
            sofar = sofar + weight(l, h, at) * product[i * HEAD : (i + 1) * HEAD]
        return sofar

    def middle(g, c, at):
        for h in heads_of(g):
            acc[spot(h, c)] = add_levels(c, at, h, range(1, top - 1))

    def last(g, c, at):
        for h in heads_of(g):
            cols = slice(h * HEAD, (h + 1) * HEAD)
            attended = add_levels(c, at, h, range(top - 1, levels))
            squares = jnp.mean(attended * attended, axis=0, keepdims=True)
            gain = jnp.concatenate([gains[cols, :]] * (CHUNK // HEAD), axis=1)
            normed = attended * lax.rsqrt(squares + EPSILON) * gain
            k[at, cols] = normed.astype(BF16).T

    def z1_arrived(s):
        z_arrived(1, s)
        z_forward(1, s)
        start("x", 1, s)
        if s == 1:
            start("c0", 1)

    def z2_arrived(s):
        z_arrived(2, s)
        z_forward(2, s)
        if s == 0:
            start("x", 2, 0)
            start("y", 2, 0)
        else:
            sides_arrived(0)
            diagonals(0)
            start("x", 2, 1)
            start("y", 2, 1)
            start("c0", 2)

    late = relays(top)

    def forward_3(s):
        def go():
            z_arrived(3, s)
            z_forward(3, s)

        return go

    def forward_3_early():
        pl.when(forwards(3))(forward_3(0))
        pl.when(jnp.logical_and(forwards(3), jnp.logical_not(late)))(forward_3(1))

    def forward_3_late():
        pl.when(jnp.logical_and(forwards(3), late))(forward_3(1))

    def z3_arrived(s):
        pl.when(jnp.logical_not(forwards(3)))(lambda: z_arrived(3, s))
        start("x", 3, s)
        start("y", 3, s)
        if s == 1:
            start("c0", 3)

    def last_of_first():
        advance(1, 3)
        for s in range(2):
            start("y", 1, s)

    def all_diagonal_0():
        diagonal_arrived(0)
        for s in range(2):
            start("dz", s)

    def all_sides_2():
        sides_arrived(2)
        diagonals(2)

    def passed_middle(g):
        for l in range(1, top - 1):
            passed(l, g)

    def passed_last(g):
        passed(top - 1, g)
        passed(top, g)

    for g in range(GROUPS):
        states(0, g)
        if g:
            advance_first(g - 1)
        states(1, g)
    advance_first(GROUPS - 1)
    start("x", 0, 1)
    gate_load.wait()
    gain_load.wait()
    for b in range(rows // HEAD):
        at = slice(b * HEAD, (b + 1) * HEAD)
        tile = gate_ref[at, :].astype(F32).T
        scale = [jnp.ones((heads, HEAD), F32)] + [
            jnp.full((heads, HEAD), flags[l].astype(F32)) for l in range(levels)
        ]
        rest = tile.shape[0] - heads * len(scale)
        if rest:
            scale.append(jnp.zeros((rest, HEAD), F32))
        gates[:, at] = tile * jnp.concatenate(scale, axis=0)
    for h in range(heads):
        cols = slice(h * HEAD, (h + 1) * HEAD)
        gains[cols, :] = jnp.broadcast_to(gain_ref[:, cols], (HEAD, HEAD)).T

    for g in range(GROUPS):
        receive("first", 1, g)
    for one in q_loads:
        one.wait()
    body(local, 0, {1: lambda: z1_arrived(0), 3: lambda: advance(1, 0)})
    body(local, 1, {2: lambda: advance(1, 1), 3: lambda: z1_arrived(1)})
    body(local, 2, {1: lambda: advance(1, 2), 3: lambda: advance(2, 0)})
    body(local, 3, {0: last_of_first, 1: lambda: z2_arrived(0), 2: lambda: advance(2, 1)})
    advance(2, 2)
    z2_arrived(1)
    advance(2, 3)
    for l in range(3, top - 1):
        for g in range(GROUPS):
            advance(l, g)
    passed_middle(0)
    body(middle, 0, {})
    forward_3_early()
    advance(top - 1, 0)
    passed_middle(1)
    body(middle, 1, {})
    advance(top - 1, 1)
    passed_middle(2)
    body(middle, 2, {})
    advance(top - 1, 2)
    passed_middle(3)
    body(middle, 3, {})
    advance(top - 1, 3)
    advance(top, 0)
    advance(top, 1)
    passed_last(0)
    body(last, 0, {1: lambda: z3_arrived(0), 2: lambda: advance(top, 2)})
    advance(top, 3)
    forward_3_late()
    passed_last(1)
    body(last, 1, {3: lambda: sides_arrived(1)})
    passed_last(2)
    body(last, 2, {3: all_diagonal_0})
    passed_last(3)
    body(last, 3, {})

    def rest_columns():
        for j in range(4, columns):
            for s in range(2):
                z_arrived(j, s)
                z_forward(j, s)
                start("x", j, s)
                start("y", j, s)
            start("c0", j)
        for j in range(4, columns):
            sides_arrived(j)
            diagonals(j)
        for j in range(4, columns):
            diagonal_arrived(j)

    def project(pieces, fresh, tasks):
        def step(c, carry):
            at = pl.ds(pl.multiple_of(c * CHUNK, CHUNK), CHUNK)
            product = None
            for planes in pieces:
                more = dot(k[at, planes], whole[planes, :])
                product = more if product is None else product + more
            acc[at, :] = product if fresh else acc[at, :] + product
            for point, task in tasks.items():
                pl.when(c == point)(task)
            return carry

        lax.fori_loop(0, chunks, step, 0)

    mine.wait()
    for kind in ("c0", "c2", "c4", "c6"):
        receive(kind, 0)
    for kind in ("c0", "c2"):
        receive(kind, 1)

    def rest_of_3():
        z3_arrived(1)
        all_sides_2()

    def all_sides_3():
        sides_arrived(3)
        diagonals(3)

    apart = splits(part)
    pieces = [plane_rows(me, 0, columns, part)]
    if apart:
        pieces.append(half_plane_rows(me, 1, columns, False, part))
    project(pieces, True, {0: rest_of_3})
    if columns > 4:
        rest_columns()
    for j in range(4, columns):
        for kind in ("c0", "c2", "c4", "c6"):
            receive(kind, j)
        project([plane_rows(me, j, columns, part)], False, {})
    for kind in ("c0", "c2"):
        receive(kind, 2)
    if apart:
        project([half_plane_rows(me, 2, columns, False, part)], False, {3: all_sides_3})
    else:
        all_sides_3()
    diagonal_arrived(1)
    for kind in ("c4", "c6"):
        receive(kind, 1)
    if apart:
        project([half_plane_rows(me, 1, columns, True, part)], False, {3: lambda: diagonal_arrived(2)})
    else:
        project([plane_rows(me, 1, columns, part)], False, {3: lambda: diagonal_arrived(2)})
    for kind in ("c0", "c2"):
        receive(kind, 3)
    if apart:
        project([half_plane_rows(me, 3, columns, False, part)], False, {})
    diagonal_arrived(3)
    for j in (2, 3):
        for kind in ("c4", "c6"):
            receive(kind, j)
    for name in ids:
        if name[0] == "stage" and name[1] >= 3:
            cond = jnp.logical_or(origin(name[1]), relays(name[1]))
        elif name[0] == "pass" and name[1] >= 3:
            cond = receives(name[1])
        elif name[0] in ("up", "down"):
            cond = has_up if name[0] == "up" else has_down
        elif name[0] == "z":
            if name[1] == 0:
                continue
            cond = forwards(name[1])
        else:
            send(name).wait_send()
            continue
        pl.when(cond)(lambda name=name: send(name).wait_send())


def project_kernel(n, part, acc_ref, normed_ref, whole_ref, out_ref):
    at = pl.ds(pl.multiple_of(pl.program_id(0) * CHUNK, CHUNK), CHUNK)
    me = lax.axis_index("ctx")
    product = acc_ref[at, :]
    for j in (2, 3):
        planes = half_plane_rows(me, j, n // 8, True, part) if splits(part) else plane_rows(me, j, n // 8, part)
        product = product + dot(normed_ref[at, planes], whole_ref[planes, :])
    out_ref[...] = product.astype(BF16)


def shards(queries, keys, values, level_gate, norm_gain, out_weight):
    n = lax.axis_size("ctx")
    rows, width = queries.shape
    heads, chunks = width // HEAD, rows // CHUNK
    levels = n.bit_length() - 1
    count = len(transfers(levels, n // 8))
    vmem = pl.BlockSpec(memory_space=pltpu.VMEM)
    hbm = pl.BlockSpec(memory_space=pltpu.HBM)
    out_width = out_weight.shape[1]
    weight_rows = n * out_weight.shape[0]
    acc, normed, whole = pl.pallas_call(
        functools.partial(kernel, n),
        out_shape=[
            pltpu.VMEM((rows, width), F32),
            pltpu.VMEM((rows, width), BF16),
            pltpu.VMEM((weight_rows, out_width), BF16),
        ],
        in_specs=[hbm] * 6,
        out_specs=[vmem] * 3,
        scratch_shapes=[
            pltpu.VMEM((rows, width), BF16),
            pltpu.VMEM((rows, width), BF16),
            pltpu.VMEM(level_gate.shape, BF16),
            pltpu.VMEM((1, width), F32),
            pltpu.VMEM((width, rows), BF16),
            pltpu.VMEM((level_gate.shape[1], rows), F32),
            pltpu.VMEM((width, HEAD), F32),
            pltpu.VMEM((chunks, heads, HEAD, HEAD), BF16),
            pltpu.VMEM((heads // 2, HEAD, HEAD), F32),
            pltpu.VMEM((levels, heads, HEAD, HEAD), BF16),
            pltpu.VMEM((heads, HEAD, HEAD), BF16),
            pltpu.VMEM((levels - 1, heads // 2, HEAD, HEAD), BF16),
            pltpu.SemaphoreType.DMA((4, max(2 * GROUPS, chunks))),
            pltpu.SemaphoreType.DMA((count,)),
            pltpu.SemaphoreType.DMA((count,)),
        ],
        compiler_params=pltpu.CompilerParams(
            collective_id=0, has_side_effects=True, vmem_limit_bytes=40 * 1024 * 1024
        ),
        name="layer",
    )(queries, keys, values, level_gate, norm_gain.reshape(1, -1), out_weight)
    return pl.pallas_call(
        functools.partial(project_kernel, n, out_weight.shape[0]),
        grid=(chunks,),
        out_shape=jax.ShapeDtypeStruct((rows, out_width), BF16),
        in_specs=[vmem] * 3,
        out_specs=pl.BlockSpec((CHUNK, out_width), lambda i: (i, 0)),
        compiler_params=pltpu.CompilerParams(vmem_limit_bytes=12 * 1024 * 1024),
        name="project",
    )(acc, normed, whole)


def solution(mesh):
    placed = (P("ctx", None), P("ctx", None), P("ctx", None), P("ctx", None), P(), P("ctx", None))
    return jax.shard_map(
        shards, mesh=mesh, in_specs=placed, out_specs=P("ctx", None), check_vma=False
    )
```

```python
import functools
import jax
import jax.numpy as jnp
from jax import lax
from jax.experimental import pallas as pl
from jax.experimental.pallas import tpu as pltpu
from jax.sharding import PartitionSpec as P

HEAD = 128
CHUNK = 256
GROUPS = 4
EPSILON = 1e-06
F32 = jnp.float32
BF16 = jnp.bfloat16
MESH = pl.DeviceIdType.MESH


def dot(a, b, dims=((1,), (0,))):
    return lax.dot_general(a, b, (dims, ((), ())), preferred_element_type=F32)


def other(me, mask):
    bit = 1
    out = me
    while bit <= mask:
        if mask & bit:
            out = out + bit * (1 - 2 * ((me // bit) % 2))
        bit *= 2
    return out


def transfers(levels, columns):
    names = [("first", i, g) for i in range(2) for g in range(GROUPS)]
    for l in range(1, levels):
        names += [(kind, l, g) for kind in ("stage", "pass") for g in range(GROUPS)]
    names += [("up", s) for s in range(2)] + [("down", s) for s in range(2)]
    names += [("z", j, s) for j in range(columns) for s in range(2)]
    names += [(kind, j, s) for kind in ("x", "y") for j in range(columns) for s in range(2)]
    names += [(kind, j) for kind in ("dx", "dy") for j in range(columns) if j != 1]
    names += [("dz", s) for s in range(2)]
    names += [(kind, j) for kind in ("c0", "c2", "c4", "c6") for j in range(columns)]
    return {name: at for at, name in enumerate(names)}


def nth_column(me, k, columns):
    column = me // 8
    if k < 2:
        return column + k * (1 - 2 * (column % 2))
    pair, step, pairs = column // 2, k // 2, columns // 2
    upper = pair // (pairs // 2)
    low = pair + upper * (pairs - 1 - 2 * pair)
    inside = (step <= 2 * low).astype(jnp.int32)
    near = low + (step + 1) // 2 * (1 - 2 * (step % 2))
    found = inside * near + (1 - inside) * step
    found = found + upper * (pairs - 1 - 2 * found)
    above = (found > pair).astype(jnp.int32)
    return 2 * found + above * (k % 2) + (1 - above) * (1 - k % 2)


def plane_rows(me, k, columns, part):
    return pl.ds(pl.multiple_of(nth_column(me, k, columns) * (8 * part), 8 * part), 8 * part)


def splits(part):
    return 4 * part % HEAD == 0


def half_plane_rows(me, k, columns, far, part):
    here = me // 4 % 2
    first = nth_column(me, k, columns) * 2 + (1 - here if far else here)
    return pl.ds(pl.multiple_of(first * (4 * part), 4 * part), 4 * part)


def kernel(n, q_hbm, k_hbm, v_hbm, gate_hbm, gain_hbm, w_hbm, acc, k, whole,
           q, v, gate_ref, gain_ref, turned, gates, gains, prefix, running, buckets, first, sends,
           load_sem, send_sem, recv_sem):
    rows, width = q.shape
    heads, chunks = width // HEAD, rows // CHUNK
    half = heads // 2
    group = half // GROUPS
    levels = n.bit_length() - 1
    columns = n // 8
    top = levels - 1
    part = w_hbm.shape[0]
    ids = transfers(levels, columns)
    me = lax.axis_index("ctx")
    core = me % 2
    column = me // 8
    flags = [(me // (1 << l)) % 2 for l in range(levels)]

    def part_of(core_bit, g):
        return pl.ds(core_bit * half + g * group, group)

    def side_of(i):
        return 1 - core if i == 0 else core

    def load(hbm, buffer, kind, at, i, g):
        sem = load_sem.at[kind, at]
        if kind == 2:
            rows_here = pl.ds(at * CHUNK, CHUNK)
            return pltpu.make_async_copy(hbm.at[rows_here], buffer.at[rows_here], sem)
        if kind == 3:
            return pltpu.make_async_copy(hbm, buffer, sem)
        wide = group * HEAD
        cols = pl.ds(pl.multiple_of(side_of(i) * (half * HEAD) + g * wide, wide), wide)
        return pltpu.make_async_copy(hbm.at[:, cols], buffer.at[:, cols], sem)

    def loads(i, g):
        at = g * 2 + i
        return load(k_hbm, k, 0, at, i, g), load(v_hbm, v, 1, at, i, g)

    has_up = column < columns - 1
    has_down = column > 0
    barrier = pltpu.get_barrier_semaphore()

    def greet(device):
        pl.semaphore_signal(barrier, inc=1, device_id=(device,), device_id_type=MESH)

    for mask in (1, 2, 4):
        greet(other(me, mask))
    pl.when(has_up)(lambda: greet(me + 8))
    pl.when(has_down)(lambda: greet(me - 8))

    for g in range(GROUPS):
        for i in range(2):
            for one in loads(i, g):
                one.start()
    gate_load = load(gate_hbm, gate_ref, 3, 1, 0, 0)
    gain_load = load(gain_hbm, gain_ref, 3, 2, 0, 0)
    gate_load.start()
    gain_load.start()
    q_loads = [load(q_hbm, q, 2, c, 0, 0) for c in range(chunks)]
    for one in q_loads:
        one.start()

    inside = has_up.astype(jnp.int32) + has_down.astype(jnp.int32)
    pl.semaphore_wait(barrier, 3 + inside)

    def z_sem(at, s):
        return ids["z", 0, 0] + 2 * at + s

    def copy(name, src, dst, device, landing=None):
        at = ids[name]
        landing = at if landing is None else landing
        return pltpu.make_async_remote_copy(
            src_ref=src, dst_ref=dst, send_sem=send_sem.at[at], recv_sem=recv_sem.at[landing],
            device_id=(device,), device_id_type=MESH,
        )

    side_width = whole.shape[1] // 2

    place_of = [nth_column(me, k, columns) for k in range(columns)]

    def block(device, side=None):
        at = pl.ds(pl.multiple_of(device * part, part), part)
        if side is None:
            return whole.at[at]
        return whole.at[at, pl.ds(side * side_width, side_width)]

    def shard(mask, k, side=None):
        return block(other(me, mask) + (place_of[k] - column) * 8, side)

    def own(side):
        return w_hbm.at[:, pl.ds(side * side_width, side_width)]

    def place(l):
        return column % (2 << (l - 3))

    def receives(l):
        return flags[l] == 1

    def origin(l):
        return place(l) == (1 << (l - 3)) - 1

    def relays(l):
        return jnp.logical_and(place(l) >= 1 << (l - 3), place(l) < (2 << (l - 3)) - 1)

    def send(name, relay=False):
        kind, j = name[:2]
        if kind == "first":
            at = part_of(side_of(j), name[2])
            return copy(name, first.at[at], buckets.at[0, at], other(me, 1))
        if kind in ("stage", "pass"):
            g = name[2]
            here = buckets.at[j, part_of(core, g)]
            if kind == "pass":
                return copy(name, here, here, other(me, 1))
            src = here if relay else sends.at[j - 1, pl.ds(g * group, group)]
            return copy(name, src, here, other(me, 1 << j) if j < 3 else me + 8)
        if kind == "dz":
            return copy(name, shard(6, 0, j), shard(6, 0, j), other(me, 8))
        if kind in ("up", "down"):
            return copy(name, own(j), shard(0, 0, j), me + 8 if kind == "up" else me - 8, z_sem(column, j))
        if kind == "z":
            s = name[2]
            at = shard(0, j, s)
            onward = 1 - 2 * (place_of[j] > column).astype(jnp.int32)
            return copy(name, at, at, me + 8 * onward, z_sem(place_of[j], s))
        if kind in ("x", "y"):
            s = name[2]
            src = own(s) if j == 0 else shard(0, j, s)
            return copy(name, src, shard(0, j, s), other(me, {"x": 2, "y": 4}[kind]))
        if kind == "dy":
            return copy(name, shard(2, j, 0), shard(2, j, 0), other(me, 4))
        if kind == "dx":
            return copy(name, shard(4, j, 1), shard(4, j, 1), other(me, 2))
        mask = int(kind[1])
        src = w_hbm if mask == 0 and j == 0 else shard(mask, j)
        return copy(name, src, shard(mask, j), other(me, 1))

    def arrival(name):
        kind, j = name[:2]
        if kind == "first":
            dst = buckets.at[0, part_of(side_of(1 - j), name[2])]
        elif kind == "stage":
            dst = buckets.at[j, part_of(core, name[2])]
        elif kind == "pass":
            dst = buckets.at[j, part_of(1 - core, name[2])]
        elif kind == "dz":
            dst = shard(6, 1, j)
        elif kind == "z":
            dst = shard(0, j, name[2])
            return copy(name, dst, dst, other(me, 1), z_sem(place_of[j], name[2]))
        elif kind in ("x", "y"):
            dst = shard({"x": 2, "y": 4}[kind], j, name[2])
        elif kind == "dy":
            dst = shard(6, j, 0)
        elif kind == "dx":
            dst = shard(6, j, 1)
        else:
            dst = shard(1 ^ int(kind[1]), j)
        return copy(name, dst, dst, other(me, 1))

    def start(*name):
        send(name).start()

    def receive(*name):
        arrival(name).wait_recv()

    mine = pltpu.make_async_copy(w_hbm, shard(0, 0), load_sem.at[3, 0])
    mine.start()
    start("x", 0, 0)
    start("y", 0, 0)
    pl.when(has_up)(lambda: start("up", 0))
    pl.when(has_down)(lambda: start("down", 0))
    start("y", 0, 1)
    pl.when(has_up)(lambda: start("up", 1))
    pl.when(has_down)(lambda: start("down", 1))
    start("c0", 0)

    for l in range(3, levels):
        @pl.when(flags[l] == 0)
        def _(l=l):
            buckets[l] = jnp.zeros(buckets.shape[1:], BF16)

    def states(i, g):
        for one in loads(i, g):
            one.wait()
        for e in range(group):
            h = side_of(i) * half + g * group + e
            cols = pl.ds(pl.multiple_of(h * HEAD, HEAD), HEAD)
            sofar = jnp.zeros((HEAD, HEAD), F32)
            for c in range(chunks):
                at = slice(c * CHUNK, (c + 1) * CHUNK)
                prefix[c, h] = sofar.astype(BF16)
                flipped = v[at, cols].T
                turned[cols, at] = flipped
                sofar = sofar + dot(flipped, k[at, cols])
            first[h] = sofar.astype(BF16)
            if i == 1:
                running[g * group + e] = sofar
        start("first", i, g)

    def send_on(l, g):
        at = pl.ds(g * group, group)

        def go():
            sends[l, at] = running[at].astype(BF16)
            start("stage", l + 1, g)

        if l + 1 < 3:
            go()
        else:
            pl.when(origin(l + 1))(go)

    def advance_first(g):
        receive("first", 0, g)
        at = pl.ds(g * group, group)
        running[at] = running[at] + buckets[0, part_of(core, g)].astype(F32)
        send_on(0, g)

    def advance(l, g):
        def arrived():
            receive("stage", l, g)
            if l >= 3:
                @pl.when(relays(l))
                def _():
                    send(("stage", l, g), relay=True).start()
            if l + 1 < levels:
                at = pl.ds(g * group, group)
                running[at] = running[at] + buckets[l, part_of(core, g)].astype(F32)

        def passing():
            start("pass", l, g)

        if l < 3:
            arrived()
        else:
            pl.when(receives(l))(arrived)
        if l + 1 < levels:
            send_on(l, g)
        if l < 3:
            passing()
        else:
            pl.when(receives(l))(passing)

    def passed(l, g):
        if l < 3:
            receive("pass", l, g)
        else:
            pl.when(receives(l))(lambda: receive("pass", l, g))

    def forwards(k):
        down = place_of[k] > column
        return jnp.logical_or(jnp.logical_and(down, has_down), jnp.logical_and(jnp.logical_not(down), has_up))

    def z_forward(k, s):
        pl.when(forwards(k))(lambda: start("z", k, s))

    def z_arrived(k, s):
        receive("z", k, s)

    def sides_arrived(j):
        for s in range(2):
            receive("x", j, s)
            receive("y", j, s)
        start("c2", j)
        start("c4", j)

    def diagonals(j):
        start("dy", j)
        start("dx", j)

    def diagonal_arrived(j):
        if j == 1:
            for s in range(2):
                receive("dz", s)
        else:
            receive("dy", j)
            receive("dx", j)
        start("c6", j)

    def heads_of(g):
        return [side * half + g * group + e for side in range(2) for e in range(group)]

    def body(function, g, tasks):
        for c in range(chunks):
            function(g, c, slice(c * CHUNK, (c + 1) * CHUNK))
            if c in tasks:
                tasks[c]()

    def weight(l, h, at):
        row = (l + 1) * heads + h
        return gates[row : row + 1, at]

    def spot(h, c):
        down, across = divmod(h * chunks, heads // 2)
        return slice(down * HEAD, (down + 1) * HEAD), slice((across + c) * CHUNK, (across + c + 1) * CHUNK)

    def local(g, c, at):
        causal = lax.broadcasted_iota(jnp.int32, (CHUNK, CHUNK), 0) <= lax.broadcasted_iota(
            jnp.int32, (CHUNK, CHUNK), 1
        )
        for h in heads_of(g):
            cols = slice(h * HEAD, (h + 1) * HEAD)
            stack = jnp.concatenate([k[at, cols], prefix[c, h], buckets[0, h]], axis=0)
            product = dot(stack, q[at, cols], ((1,), (1,)))
            scores = jnp.where(causal, product[:CHUNK], 0.0).astype(BF16)
            mixed = dot(turned[cols, at], scores) + product[CHUNK : CHUNK + HEAD]
            acc[spot(h, c)] = mixed * weight(-1, h, at) + product[CHUNK + HEAD :] * weight(0, h, at)

    def add_levels(c, at, h, wanted):
        cols = slice(h * HEAD, (h + 1) * HEAD)
        stack = jnp.concatenate([buckets[l, h] for l in wanted], axis=0)
        product = dot(stack, q[at, cols], ((1,), (1,)))
        sofar = acc[spot(h, c)]
        for i, l in enumerate(wanted):
            sofar = sofar + weight(l, h, at) * product[i * HEAD : (i + 1) * HEAD]
        return sofar

    def middle(g, c, at):
        for h in heads_of(g):
            acc[spot(h, c)] = add_levels(c, at, h, range(1, top - 1))

    def last(g, c, at):
        for h in heads_of(g):
            cols = slice(h * HEAD, (h + 1) * HEAD)
            attended = add_levels(c, at, h, range(top - 1, levels))
            squares = jnp.mean(attended * attended, axis=0, keepdims=True)
            gain = jnp.concatenate([gains[cols, :]] * (CHUNK // HEAD), axis=1)
            normed = attended * lax.rsqrt(squares + EPSILON) * gain
            k[at, cols] = normed.astype(BF16).T

    def z1_arrived(s):
        z_arrived(1, s)
        z_forward(1, s)

        @pl.when(forwards(2))
        def _():
            z_arrived(2, s)
            z_forward(2, s)

        start("x", 1, s)
        if s == 1:
            start("c0", 1)

    def z2_arrived(s):
        pl.when(jnp.logical_not(forwards(2)))(lambda: z_arrived(2, s))
        if s == 0:
            start("x", 2, 0)
            start("y", 2, 0)
        else:
            sides_arrived(0)
            diagonals(0)
            start("x", 2, 1)
            start("y", 2, 1)
            start("c0", 2)

    late = relays(top)

    def forward_3(s):
        def go():
            z_arrived(3, s)
            z_forward(3, s)

        return go

    def forward_3_early():
        for s in range(2):
            pl.when(jnp.logical_and(forwards(3), jnp.logical_not(late)))(forward_3(s))

    def forward_3_late(s):
        pl.when(jnp.logical_and(forwards(3), late))(forward_3(s))

    def z3_arrived(s):
        pl.when(jnp.logical_not(forwards(3)))(lambda: z_arrived(3, s))
        start("x", 3, s)
        start("y", 3, s)
        if s == 1:
            start("c0", 3)

    def last_of_first():
        advance(1, 3)
        for s in range(2):
            start("y", 1, s)

    def all_diagonal_0():
        diagonal_arrived(0)
        for s in range(2):
            start("dz", s)

    def all_sides_2():
        sides_arrived(2)
        diagonals(2)

    def passed_middle(g):
        for l in range(1, top - 1):
            passed(l, g)

    def passed_last(g):
        passed(top - 1, g)
        passed(top, g)

    for g in range(GROUPS):
        states(0, g)
        if g:
            advance_first(g - 1)
        states(1, g)
    advance_first(GROUPS - 1)
    start("x", 0, 1)
    gate_load.wait()
    gain_load.wait()
    for b in range(rows // HEAD):
        at = slice(b * HEAD, (b + 1) * HEAD)
        tile = gate_ref[at, :].astype(F32).T
        scale = [jnp.ones((heads, HEAD), F32)] + [
            jnp.full((heads, HEAD), flags[l].astype(F32)) for l in range(levels)
        ]
        rest = tile.shape[0] - heads * len(scale)
        if rest:
            scale.append(jnp.zeros((rest, HEAD), F32))
        gates[:, at] = tile * jnp.concatenate(scale, axis=0)
    for h in range(heads):
        cols = slice(h * HEAD, (h + 1) * HEAD)
        gains[cols, :] = jnp.broadcast_to(gain_ref[:, cols], (HEAD, HEAD)).T

    for g in range(GROUPS):
        receive("first", 1, g)
    for one in q_loads:
        one.wait()
    body(local, 0, {1: lambda: z1_arrived(0), 3: lambda: advance(1, 0)})
    body(local, 1, {2: lambda: advance(1, 1), 3: lambda: z1_arrived(1)})
    body(local, 2, {1: lambda: advance(1, 2), 3: lambda: advance(2, 0)})
    body(local, 3, {0: last_of_first, 1: lambda: z2_arrived(0), 2: lambda: advance(2, 1)})
    advance(2, 2)
    z2_arrived(1)
    advance(2, 3)
    for l in range(3, top - 1):
        for g in range(GROUPS):
            advance(l, g)
    passed_middle(0)
    body(middle, 0, {})
    forward_3_early()
    advance(top - 1, 0)
    passed_middle(1)
    body(middle, 1, {})
    advance(top - 1, 1)
    passed_middle(2)
    body(middle, 2, {})
    advance(top - 1, 2)
    passed_middle(3)
    body(middle, 3, {})
    advance(top - 1, 3)
    advance(top, 0)
    advance(top, 1)
    passed_last(0)
    body(last, 0, {2: lambda: advance(top, 2)})
    advance(top, 3)
    forward_3_late(0)
    forward_3_late(1)
    passed_last(1)
    body(last, 1, {3: lambda: sides_arrived(1)})
    passed_last(2)
    body(last, 2, {1: lambda: z3_arrived(0), 3: all_diagonal_0})
    passed_last(3)
    body(last, 3, {})

    def rest_columns():
        for j in range(4, columns):
            for s in range(2):
                z_arrived(j, s)
                z_forward(j, s)
                start("x", j, s)
                start("y", j, s)
            start("c0", j)
        for j in range(4, columns):
            sides_arrived(j)
            diagonals(j)
        for j in range(4, columns):
            diagonal_arrived(j)

    def project(pieces, fresh, tasks):
        def step(c, carry):
            at = pl.ds(pl.multiple_of(c * CHUNK, CHUNK), CHUNK)
            product = None
            for planes in pieces:
                more = dot(k[at, planes], whole[planes, :])
                product = more if product is None else product + more
            acc[at, :] = product if fresh else acc[at, :] + product
            for point, task in tasks.items():
                pl.when(c == point)(task)
            return carry

        lax.fori_loop(0, chunks, step, 0)

    mine.wait()
    for kind in ("c0", "c2", "c4", "c6"):
        receive(kind, 0)
    for kind in ("c0", "c2"):
        receive(kind, 1)

    def rest_of_3():
        z3_arrived(1)
        all_sides_2()

    def all_sides_3():
        sides_arrived(3)
        diagonals(3)

    apart = splits(part)
    pieces = [plane_rows(me, 0, columns, part)]
    if apart:
        pieces.append(half_plane_rows(me, 1, columns, False, part))
    project(pieces, True, {0: rest_of_3})
    if columns > 4:
        rest_columns()
    for j in range(4, columns):
        for kind in ("c0", "c2", "c4", "c6"):
            receive(kind, j)
        project([plane_rows(me, j, columns, part)], False, {})
    for kind in ("c0", "c2"):
        receive(kind, 2)
    if apart:
        project([half_plane_rows(me, 2, columns, False, part)], False, {3: all_sides_3})
    else:
        all_sides_3()
    diagonal_arrived(1)
    for kind in ("c4", "c6"):
        receive(kind, 1)
    if apart:
        project([half_plane_rows(me, 1, columns, True, part)], False, {3: lambda: diagonal_arrived(2)})
    else:
        project([plane_rows(me, 1, columns, part)], False, {3: lambda: diagonal_arrived(2)})
    for kind in ("c0", "c2"):
        receive(kind, 3)
    if apart:
        project([half_plane_rows(me, 3, columns, False, part)], False, {})
    diagonal_arrived(3)
    for j in (2, 3):
        for kind in ("c4", "c6"):
            receive(kind, j)
    for name in ids:
        if name[0] == "stage" and name[1] >= 3:
            cond = jnp.logical_or(origin(name[1]), relays(name[1]))
        elif name[0] == "pass" and name[1] >= 3:
            cond = receives(name[1])
        elif name[0] in ("up", "down"):
            cond = has_up if name[0] == "up" else has_down
        elif name[0] == "z":
            if name[1] == 0:
                continue
            cond = forwards(name[1])
        else:
            send(name).wait_send()
            continue
        pl.when(cond)(lambda name=name: send(name).wait_send())


def project_kernel(n, part, acc_ref, normed_ref, whole_ref, out_ref):
    at = pl.ds(pl.multiple_of(pl.program_id(0) * CHUNK, CHUNK), CHUNK)
    me = lax.axis_index("ctx")
    product = acc_ref[at, :]
    for j in (2, 3):
        planes = half_plane_rows(me, j, n // 8, True, part) if splits(part) else plane_rows(me, j, n // 8, part)
        product = product + dot(normed_ref[at, planes], whole_ref[planes, :])
    out_ref[...] = product.astype(BF16)


def shards(queries, keys, values, level_gate, norm_gain, out_weight):
    n = lax.axis_size("ctx")
    rows, width = queries.shape
    heads, chunks = width // HEAD, rows // CHUNK
    levels = n.bit_length() - 1
    count = len(transfers(levels, n // 8))
    vmem = pl.BlockSpec(memory_space=pltpu.VMEM)
    hbm = pl.BlockSpec(memory_space=pltpu.HBM)
    out_width = out_weight.shape[1]
    weight_rows = n * out_weight.shape[0]
    acc, normed, whole = pl.pallas_call(
        functools.partial(kernel, n),
        out_shape=[
            pltpu.VMEM((rows, width), F32),
            pltpu.VMEM((rows, width), BF16),
            pltpu.VMEM((weight_rows, out_width), BF16),
        ],
        in_specs=[hbm] * 6,
        out_specs=[vmem] * 3,
        scratch_shapes=[
            pltpu.VMEM((rows, width), BF16),
            pltpu.VMEM((rows, width), BF16),
            pltpu.VMEM(level_gate.shape, BF16),
            pltpu.VMEM((1, width), F32),
            pltpu.VMEM((width, rows), BF16),
            pltpu.VMEM((level_gate.shape[1], rows), F32),
            pltpu.VMEM((width, HEAD), F32),
            pltpu.VMEM((chunks, heads, HEAD, HEAD), BF16),
            pltpu.VMEM((heads // 2, HEAD, HEAD), F32),
            pltpu.VMEM((levels, heads, HEAD, HEAD), BF16),
            pltpu.VMEM((heads, HEAD, HEAD), BF16),
            pltpu.VMEM((levels - 1, heads // 2, HEAD, HEAD), BF16),
            pltpu.SemaphoreType.DMA((4, max(2 * GROUPS, chunks))),
            pltpu.SemaphoreType.DMA((count,)),
            pltpu.SemaphoreType.DMA((count,)),
        ],
        compiler_params=pltpu.CompilerParams(
            collective_id=0, has_side_effects=True, vmem_limit_bytes=40 * 1024 * 1024
        ),
        name="layer",
    )(queries, keys, values, level_gate, norm_gain.reshape(1, -1), out_weight)
    return pl.pallas_call(
        functools.partial(project_kernel, n, out_weight.shape[0]),
        grid=(chunks,),
        out_shape=jax.ShapeDtypeStruct((rows, out_width), BF16),
        in_specs=[vmem] * 3,
        out_specs=pl.BlockSpec((CHUNK, out_width), lambda i: (i, 0)),
        compiler_params=pltpu.CompilerParams(vmem_limit_bytes=12 * 1024 * 1024),
        name="project",
    )(acc, normed, whole)


def solution(mesh):
    placed = (P("ctx", None), P("ctx", None), P("ctx", None), P("ctx", None), P(), P("ctx", None))
    return jax.shard_map(
        shards, mesh=mesh, in_specs=placed, out_specs=P("ctx", None), check_vma=False
    )
```

```python
import functools
import jax
import jax.numpy as jnp
from jax import lax
from jax.experimental import pallas as pl
from jax.experimental.pallas import tpu as pltpu
from jax.sharding import PartitionSpec as P

HEAD = 128
CHUNK = 256
GROUPS = 4
EPSILON = 1e-06
F32 = jnp.float32
BF16 = jnp.bfloat16
MESH = pl.DeviceIdType.MESH


def dot(a, b, dims=((1,), (0,))):
    return lax.dot_general(a, b, (dims, ((), ())), preferred_element_type=F32)


def other(me, mask):
    bit = 1
    out = me
    while bit <= mask:
        if mask & bit:
            out = out + bit * (1 - 2 * ((me // bit) % 2))
        bit *= 2
    return out


def transfers(levels, columns):
    names = [("first", i, g) for i in range(2) for g in range(GROUPS)]
    for l in range(1, levels):
        names += [(kind, l, g) for kind in ("stage", "pass") for g in range(GROUPS)]
    names += [("up", s) for s in range(2)] + [("down", s) for s in range(2)]
    names += [("z", j, s) for j in range(columns) for s in range(2)]
    names += [(kind, j, s) for kind in ("x", "y") for j in range(columns) for s in range(2)]
    names += [(kind, j) for kind in ("dx", "dy") for j in range(columns) if j != 1]
    names += [("dz", s) for s in range(2)]
    names += [(kind, j) for kind in ("c0", "c2", "c4", "c6") for j in range(columns)]
    return {name: at for at, name in enumerate(names)}


def nth_column(me, k, columns):
    column = me // 8
    if k < 2:
        return column + k * (1 - 2 * (column % 2))
    pair, step, pairs = column // 2, k // 2, columns // 2
    upper = pair // (pairs // 2)
    low = pair + upper * (pairs - 1 - 2 * pair)
    inside = (step <= 2 * low).astype(jnp.int32)
    near = low + (step + 1) // 2 * (1 - 2 * (step % 2))
    found = inside * near + (1 - inside) * step
    found = found + upper * (pairs - 1 - 2 * found)
    above = (found > pair).astype(jnp.int32)
    return 2 * found + above * (k % 2) + (1 - above) * (1 - k % 2)


def plane_rows(me, k, columns, part):
    return pl.ds(pl.multiple_of(nth_column(me, k, columns) * (8 * part), 8 * part), 8 * part)


def splits(part):
    return 4 * part % HEAD == 0


def half_plane_rows(me, k, columns, far, part):
    here = me // 4 % 2
    first = nth_column(me, k, columns) * 2 + (1 - here if far else here)
    return pl.ds(pl.multiple_of(first * (4 * part), 4 * part), 4 * part)


def kernel(n, q_hbm, k_hbm, v_hbm, gate_hbm, gain_hbm, w_hbm, acc, k, whole,
           q, v, gate_ref, gain_ref, turned, gates, gains, prefix, running, buckets, first, sends,
           load_sem, send_sem, recv_sem):
    rows, width = q.shape
    heads, chunks = width // HEAD, rows // CHUNK
    half = heads // 2
    group = half // GROUPS
    levels = n.bit_length() - 1
    columns = n // 8
    top = levels - 1
    part = w_hbm.shape[0]
    ids = transfers(levels, columns)
    me = lax.axis_index("ctx")
    core = me % 2
    column = me // 8
    flags = [(me // (1 << l)) % 2 for l in range(levels)]

    def part_of(core_bit, g):
        return pl.ds(core_bit * half + g * group, group)

    def side_of(i):
        return 1 - core if i == 0 else core

    def load(hbm, buffer, kind, at, i, g):
        sem = load_sem.at[kind, at]
        if kind == 2:
            rows_here = pl.ds(at * CHUNK, CHUNK)
            return pltpu.make_async_copy(hbm.at[rows_here], buffer.at[rows_here], sem)
        if kind == 3:
            return pltpu.make_async_copy(hbm, buffer, sem)
        wide = group * HEAD
        cols = pl.ds(pl.multiple_of(side_of(i) * (half * HEAD) + g * wide, wide), wide)
        return pltpu.make_async_copy(hbm.at[:, cols], buffer.at[:, cols], sem)

    def loads(i, g):
        at = g * 2 + i
        return load(k_hbm, k, 0, at, i, g), load(v_hbm, v, 1, at, i, g)

    has_up = column < columns - 1
    has_down = column > 0
    barrier = pltpu.get_barrier_semaphore()

    def greet(device):
        pl.semaphore_signal(barrier, inc=1, device_id=(device,), device_id_type=MESH)

    for mask in (1, 2, 4):
        greet(other(me, mask))
    pl.when(has_up)(lambda: greet(me + 8))
    pl.when(has_down)(lambda: greet(me - 8))

    for g in range(GROUPS):
        for i in range(2):
            for one in loads(i, g):
                one.start()
    gate_load = load(gate_hbm, gate_ref, 3, 1, 0, 0)
    gain_load = load(gain_hbm, gain_ref, 3, 2, 0, 0)
    gate_load.start()
    gain_load.start()
    q_loads = [load(q_hbm, q, 2, c, 0, 0) for c in range(chunks)]
    for one in q_loads:
        one.start()

    inside = has_up.astype(jnp.int32) + has_down.astype(jnp.int32)
    pl.semaphore_wait(barrier, 3 + inside)

    def z_sem(at, s):
        return ids["z", 0, 0] + 2 * at + s

    def copy(name, src, dst, device, landing=None):
        at = ids[name]
        landing = at if landing is None else landing
        return pltpu.make_async_remote_copy(
            src_ref=src, dst_ref=dst, send_sem=send_sem.at[at], recv_sem=recv_sem.at[landing],
            device_id=(device,), device_id_type=MESH,
        )

    side_width = whole.shape[1] // 2

    place_of = [nth_column(me, k, columns) for k in range(columns)]

    def block(device, side=None):
        at = pl.ds(pl.multiple_of(device * part, part), part)
        if side is None:
            return whole.at[at]
        return whole.at[at, pl.ds(side * side_width, side_width)]

    def shard(mask, k, side=None):
        return block(other(me, mask) + (place_of[k] - column) * 8, side)

    def own(side):
        return w_hbm.at[:, pl.ds(side * side_width, side_width)]

    def place(l):
        return column % (2 << (l - 3))

    def receives(l):
        return flags[l] == 1

    def origin(l):
        return place(l) == (1 << (l - 3)) - 1

    def relays(l):
        return jnp.logical_and(place(l) >= 1 << (l - 3), place(l) < (2 << (l - 3)) - 1)

    def send(name, relay=False):
        kind, j = name[:2]
        if kind == "first":
            at = part_of(side_of(j), name[2])
            return copy(name, first.at[at], buckets.at[0, at], other(me, 1))
        if kind in ("stage", "pass"):
            g = name[2]
            here = buckets.at[j, part_of(core, g)]
            if kind == "pass":
                return copy(name, here, here, other(me, 1))
            src = here if relay else sends.at[j - 1, pl.ds(g * group, group)]
            return copy(name, src, here, other(me, 1 << j) if j < 3 else me + 8)
        if kind == "dz":
            return copy(name, shard(6, 0, j), shard(6, 0, j), other(me, 8))
        if kind in ("up", "down"):
            return copy(name, own(j), shard(0, 0, j), me + 8 if kind == "up" else me - 8, z_sem(column, j))
        if kind == "z":
            s = name[2]
            at = shard(0, j, s)
            onward = 1 - 2 * (place_of[j] > column).astype(jnp.int32)
            return copy(name, at, at, me + 8 * onward, z_sem(place_of[j], s))
        if kind in ("x", "y"):
            s = name[2]
            src = own(s) if j == 0 else shard(0, j, s)
            return copy(name, src, shard(0, j, s), other(me, {"x": 2, "y": 4}[kind]))
        if kind == "dy":
            return copy(name, shard(2, j, 0), shard(2, j, 0), other(me, 4))
        if kind == "dx":
            return copy(name, shard(4, j, 1), shard(4, j, 1), other(me, 2))
        mask = int(kind[1])
        src = w_hbm if mask == 0 and j == 0 else shard(mask, j)
        return copy(name, src, shard(mask, j), other(me, 1))

    def arrival(name):
        kind, j = name[:2]
        if kind == "first":
            dst = buckets.at[0, part_of(side_of(1 - j), name[2])]
        elif kind == "stage":
            dst = buckets.at[j, part_of(core, name[2])]
        elif kind == "pass":
            dst = buckets.at[j, part_of(1 - core, name[2])]
        elif kind == "dz":
            dst = shard(6, 1, j)
        elif kind == "z":
            dst = shard(0, j, name[2])
            return copy(name, dst, dst, other(me, 1), z_sem(place_of[j], name[2]))
        elif kind in ("x", "y"):
            dst = shard({"x": 2, "y": 4}[kind], j, name[2])
        elif kind == "dy":
            dst = shard(6, j, 0)
        elif kind == "dx":
            dst = shard(6, j, 1)
        else:
            dst = shard(1 ^ int(kind[1]), j)
        return copy(name, dst, dst, other(me, 1))

    def start(*name):
        send(name).start()

    def receive(*name):
        arrival(name).wait_recv()

    mine = pltpu.make_async_copy(w_hbm, shard(0, 0), load_sem.at[3, 0])
    mine.start()
    start("x", 0, 0)
    start("y", 0, 0)
    pl.when(has_up)(lambda: start("up", 0))
    pl.when(has_down)(lambda: start("down", 0))
    start("y", 0, 1)
    pl.when(has_up)(lambda: start("up", 1))
    pl.when(has_down)(lambda: start("down", 1))
    start("c0", 0)

    for l in range(3, levels):
        @pl.when(flags[l] == 0)
        def _(l=l):
            buckets[l] = jnp.zeros(buckets.shape[1:], BF16)

    def states(i, g):
        for one in loads(i, g):
            one.wait()
        for e in range(group):
            h = side_of(i) * half + g * group + e
            cols = pl.ds(pl.multiple_of(h * HEAD, HEAD), HEAD)
            sofar = jnp.zeros((HEAD, HEAD), F32)
            for c in range(chunks):
                at = slice(c * CHUNK, (c + 1) * CHUNK)
                prefix[c, h] = sofar.astype(BF16)
                flipped = v[at, cols].T
                turned[cols, at] = flipped
                sofar = sofar + dot(flipped, k[at, cols])
            first[h] = sofar.astype(BF16)
            if i == 1:
                running[g * group + e] = sofar
        start("first", i, g)

    def send_on(l, g):
        at = pl.ds(g * group, group)

        def go():
            sends[l, at] = running[at].astype(BF16)
            start("stage", l + 1, g)

        if l + 1 < 3:
            go()
        else:
            pl.when(origin(l + 1))(go)

    def advance_first(g):
        receive("first", 0, g)
        at = pl.ds(g * group, group)
        running[at] = running[at] + buckets[0, part_of(core, g)].astype(F32)
        send_on(0, g)

    def advance(l, g):
        def arrived():
            receive("stage", l, g)
            if l >= 3:
                @pl.when(relays(l))
                def _():
                    send(("stage", l, g), relay=True).start()
            if l + 1 < levels:
                at = pl.ds(g * group, group)
                running[at] = running[at] + buckets[l, part_of(core, g)].astype(F32)

        def passing():
            start("pass", l, g)

        if l < 3:
            arrived()
        else:
            pl.when(receives(l))(arrived)
        if l + 1 < levels:
            send_on(l, g)
        if l < 3:
            passing()
        else:
            pl.when(receives(l))(passing)

    def passed(l, g):
        if l < 3:
            receive("pass", l, g)
        else:
            pl.when(receives(l))(lambda: receive("pass", l, g))

    def forwards(k):
        down = place_of[k] > column
        return jnp.logical_or(jnp.logical_and(down, has_down), jnp.logical_and(jnp.logical_not(down), has_up))

    def z_forward(k, s):
        pl.when(forwards(k))(lambda: start("z", k, s))

    def z_arrived(k, s):
        receive("z", k, s)

    def sides_arrived(j):
        for s in range(2):
            receive("x", j, s)
            receive("y", j, s)
        start("c2", j)
        start("c4", j)

    def diagonals(j):
        start("dy", j)
        start("dx", j)

    def diagonal_arrived(j):
        if j == 1:
            for s in range(2):
                receive("dz", s)
        else:
            receive("dy", j)
            receive("dx", j)
        start("c6", j)

    def heads_of(g):
        return [side * half + g * group + e for side in range(2) for e in range(group)]

    def body(function, g, tasks):
        for c in range(chunks):
            function(g, c, slice(c * CHUNK, (c + 1) * CHUNK))
            if c in tasks:
                tasks[c]()

    def weight(l, h, at):
        row = (l + 1) * heads + h
        return gates[row : row + 1, at]

    def spot(h, c):
        down, across = divmod(h * chunks, heads // 2)
        return slice(down * HEAD, (down + 1) * HEAD), slice((across + c) * CHUNK, (across + c + 1) * CHUNK)

    def local(g, c, at):
        causal = lax.broadcasted_iota(jnp.int32, (CHUNK, CHUNK), 0) <= lax.broadcasted_iota(
            jnp.int32, (CHUNK, CHUNK), 1
        )
        for h in heads_of(g):
            cols = slice(h * HEAD, (h + 1) * HEAD)
            stack = jnp.concatenate([k[at, cols], prefix[c, h], buckets[0, h]], axis=0)
            product = dot(stack, q[at, cols], ((1,), (1,)))
            scores = jnp.where(causal, product[:CHUNK], 0.0).astype(BF16)
            mixed = dot(turned[cols, at], scores) + product[CHUNK : CHUNK + HEAD]
            acc[spot(h, c)] = mixed * weight(-1, h, at) + product[CHUNK + HEAD :] * weight(0, h, at)

    def add_levels(c, at, h, wanted):
        cols = slice(h * HEAD, (h + 1) * HEAD)
        stack = jnp.concatenate([buckets[l, h] for l in wanted], axis=0)
        product = dot(stack, q[at, cols], ((1,), (1,)))
        sofar = acc[spot(h, c)]
        for i, l in enumerate(wanted):
            sofar = sofar + weight(l, h, at) * product[i * HEAD : (i + 1) * HEAD]
        return sofar

    def middle(g, c, at):
        for h in heads_of(g):
            acc[spot(h, c)] = add_levels(c, at, h, range(1, top - 1))

    def last(g, c, at):
        for h in heads_of(g):
            cols = slice(h * HEAD, (h + 1) * HEAD)
            attended = add_levels(c, at, h, range(top - 1, levels))
            squares = jnp.mean(attended * attended, axis=0, keepdims=True)
            gain = jnp.concatenate([gains[cols, :]] * (CHUNK // HEAD), axis=1)
            normed = attended * lax.rsqrt(squares + EPSILON) * gain
            k[at, cols] = normed.astype(BF16).T

    def z1_arrived(s):
        z_arrived(1, s)
        z_forward(1, s)

        @pl.when(forwards(2))
        def _():
            z_arrived(2, s)
            z_forward(2, s)

        start("x", 1, s)
        if s == 1:
            start("c0", 1)

    def z2_arrived(s):
        pl.when(jnp.logical_not(forwards(2)))(lambda: z_arrived(2, s))
        if s == 0:
            start("x", 2, 0)
            start("y", 2, 0)
        else:
            sides_arrived(0)
            diagonals(0)
            start("x", 2, 1)
            start("y", 2, 1)
            start("c0", 2)

    late = relays(top)

    def forward_3(s):
        def go():
            z_arrived(3, s)
            z_forward(3, s)

        return go

    def forward_3_early():
        for s in range(2):
            pl.when(jnp.logical_and(forwards(3), jnp.logical_not(late)))(forward_3(s))

    def forward_3_late(s):
        pl.when(jnp.logical_and(forwards(3), late))(forward_3(s))

    def z3_arrived(s):
        pl.when(jnp.logical_not(forwards(3)))(lambda: z_arrived(3, s))
        start("x", 3, s)
        start("y", 3, s)
        if s == 1:
            start("c0", 3)

    def last_of_first():
        advance(1, 3)
        for s in range(2):
            start("y", 1, s)

    def all_diagonal_0():
        diagonal_arrived(0)
        for s in range(2):
            start("dz", s)

    def all_sides_2():
        sides_arrived(2)
        diagonals(2)

    def passed_middle(g):
        for l in range(1, top - 1):
            passed(l, g)

    def passed_last(g):
        passed(top - 1, g)
        passed(top, g)

    for g in range(GROUPS):
        states(0, g)
        if g:
            advance_first(g - 1)
        states(1, g)
    advance_first(GROUPS - 1)
    start("x", 0, 1)
    gate_load.wait()
    gain_load.wait()
    for b in range(rows // HEAD):
        at = slice(b * HEAD, (b + 1) * HEAD)
        tile = gate_ref[at, :].astype(F32).T
        scale = [jnp.ones((heads, HEAD), F32)] + [
            jnp.full((heads, HEAD), flags[l].astype(F32)) for l in range(levels)
        ]
        rest = tile.shape[0] - heads * len(scale)
        if rest:
            scale.append(jnp.zeros((rest, HEAD), F32))
        gates[:, at] = tile * jnp.concatenate(scale, axis=0)
    for h in range(heads):
        cols = slice(h * HEAD, (h + 1) * HEAD)
        gains[cols, :] = jnp.broadcast_to(gain_ref[:, cols], (HEAD, HEAD)).T

    for g in range(GROUPS):
        receive("first", 1, g)
    for one in q_loads:
        one.wait()
    body(local, 0, {1: lambda: z1_arrived(0), 3: lambda: advance(1, 0)})
    body(local, 1, {2: lambda: advance(1, 1), 3: lambda: z1_arrived(1)})
    body(local, 2, {1: lambda: advance(1, 2), 3: lambda: advance(2, 0)})
    body(local, 3, {0: last_of_first, 1: lambda: z2_arrived(0), 2: lambda: advance(2, 1)})
    advance(2, 2)
    z2_arrived(1)
    advance(2, 3)
    for l in range(3, top - 1):
        for g in range(GROUPS):
            advance(l, g)
    passed_middle(0)
    body(middle, 0, {})
    forward_3_early()
    advance(top - 1, 0)
    passed_middle(1)
    body(middle, 1, {})
    advance(top - 1, 1)
    passed_middle(2)
    body(middle, 2, {})
    advance(top - 1, 2)
    passed_middle(3)
    body(middle, 3, {})
    advance(top - 1, 3)
    advance(top, 0)
    advance(top, 1)
    passed_last(0)
    body(last, 0, {2: lambda: advance(top, 2)})
    advance(top, 3)
    forward_3_late(0)
    forward_3_late(1)
    passed_last(1)
    body(last, 1, {3: lambda: sides_arrived(1)})
    passed_last(2)
    body(last, 2, {1: lambda: z3_arrived(0), 3: all_diagonal_0})
    passed_last(3)
    body(last, 3, {})

    def rest_columns():
        for j in range(4, columns):
            for s in range(2):
                z_arrived(j, s)
                z_forward(j, s)
                start("x", j, s)
                start("y", j, s)
            start("c0", j)
        for j in range(4, columns):
            sides_arrived(j)
            diagonals(j)
        for j in range(4, columns):
            diagonal_arrived(j)

    def project(pieces, fresh, tasks):
        wide = whole.shape[1] // chunks

        def step(c, carry):
            cols = pl.ds(pl.multiple_of(c * wide, wide), wide)
            product = None
            for planes in pieces:
                more = dot(k[:, planes], whole[planes, cols])
                product = more if product is None else product + more
            acc[:, cols] = product if fresh else acc[:, cols] + product
            for point, task in tasks.items():
                pl.when(c == point)(task)
            return carry

        lax.fori_loop(0, chunks, step, 0)

    mine.wait()
    for kind in ("c0", "c2", "c4", "c6"):
        receive(kind, 0)
    for kind in ("c0", "c2"):
        receive(kind, 1)

    def rest_of_3():
        z3_arrived(1)
        all_sides_2()

    def all_sides_3():
        sides_arrived(3)
        diagonals(3)

    apart = splits(part)
    pieces = [plane_rows(me, 0, columns, part)]
    if apart:
        pieces.append(half_plane_rows(me, 1, columns, False, part))
    project(pieces, True, {0: rest_of_3})
    if columns > 4:
        rest_columns()
    for j in range(4, columns):
        for kind in ("c0", "c2", "c4", "c6"):
            receive(kind, j)
        project([plane_rows(me, j, columns, part)], False, {})
    for kind in ("c0", "c2"):
        receive(kind, 2)
    if apart:
        project([half_plane_rows(me, 2, columns, False, part)], False, {3: all_sides_3})
    else:
        all_sides_3()
    diagonal_arrived(1)
    for kind in ("c4", "c6"):
        receive(kind, 1)
    if apart:
        project([half_plane_rows(me, 1, columns, True, part)], False, {3: lambda: diagonal_arrived(2)})
    else:
        project([plane_rows(me, 1, columns, part)], False, {3: lambda: diagonal_arrived(2)})
    for kind in ("c0", "c2"):
        receive(kind, 3)
    if apart:
        project([half_plane_rows(me, 3, columns, False, part)], False, {})
    diagonal_arrived(3)
    for j in (2, 3):
        for kind in ("c4", "c6"):
            receive(kind, j)
    for name in ids:
        if name[0] == "stage" and name[1] >= 3:
            cond = jnp.logical_or(origin(name[1]), relays(name[1]))
        elif name[0] == "pass" and name[1] >= 3:
            cond = receives(name[1])
        elif name[0] in ("up", "down"):
            cond = has_up if name[0] == "up" else has_down
        elif name[0] == "z":
            if name[1] == 0:
                continue
            cond = forwards(name[1])
        else:
            send(name).wait_send()
            continue
        pl.when(cond)(lambda name=name: send(name).wait_send())


def project_kernel(n, part, acc_ref, normed_ref, whole_ref, out_ref):
    step = out_ref.shape[0]
    at = pl.ds(pl.multiple_of(pl.program_id(0) * step, step), step)
    me = lax.axis_index("ctx")
    product = acc_ref[at, :]
    for j in (2, 3):
        planes = half_plane_rows(me, j, n // 8, True, part) if splits(part) else plane_rows(me, j, n // 8, part)
        product = product + dot(normed_ref[at, planes], whole_ref[planes, :])
    out_ref[...] = product.astype(BF16)


def shards(queries, keys, values, level_gate, norm_gain, out_weight):
    n = lax.axis_size("ctx")
    rows, width = queries.shape
    heads, chunks = width // HEAD, rows // CHUNK
    levels = n.bit_length() - 1
    count = len(transfers(levels, n // 8))
    vmem = pl.BlockSpec(memory_space=pltpu.VMEM)
    hbm = pl.BlockSpec(memory_space=pltpu.HBM)
    out_width = out_weight.shape[1]
    weight_rows = n * out_weight.shape[0]
    acc, normed, whole = pl.pallas_call(
        functools.partial(kernel, n),
        out_shape=[
            pltpu.VMEM((rows, width), F32),
            pltpu.VMEM((rows, width), BF16),
            pltpu.VMEM((weight_rows, out_width), BF16),
        ],
        in_specs=[hbm] * 6,
        out_specs=[vmem] * 3,
        scratch_shapes=[
            pltpu.VMEM((rows, width), BF16),
            pltpu.VMEM((rows, width), BF16),
            pltpu.VMEM(level_gate.shape, BF16),
            pltpu.VMEM((1, width), F32),
            pltpu.VMEM((width, rows), BF16),
            pltpu.VMEM((level_gate.shape[1], rows), F32),
            pltpu.VMEM((width, HEAD), F32),
            pltpu.VMEM((chunks, heads, HEAD, HEAD), BF16),
            pltpu.VMEM((heads // 2, HEAD, HEAD), F32),
            pltpu.VMEM((levels, heads, HEAD, HEAD), BF16),
            pltpu.VMEM((heads, HEAD, HEAD), BF16),
            pltpu.VMEM((levels - 1, heads // 2, HEAD, HEAD), BF16),
            pltpu.SemaphoreType.DMA((4, max(2 * GROUPS, chunks))),
            pltpu.SemaphoreType.DMA((count,)),
            pltpu.SemaphoreType.DMA((count,)),
        ],
        compiler_params=pltpu.CompilerParams(
            collective_id=0, has_side_effects=True, vmem_limit_bytes=40 * 1024 * 1024
        ),
        name="layer",
    )(queries, keys, values, level_gate, norm_gain.reshape(1, -1), out_weight)
    step = rows // 2
    return pl.pallas_call(
        functools.partial(project_kernel, n, out_weight.shape[0]),
        grid=(rows // step,),
        out_shape=jax.ShapeDtypeStruct((rows, out_width), BF16),
        in_specs=[vmem] * 3,
        out_specs=pl.BlockSpec((step, out_width), lambda i: (i, 0)),
        compiler_params=pltpu.CompilerParams(vmem_limit_bytes=16 * 1024 * 1024),
        name="project",
    )(acc, normed, whole)


def solution(mesh):
    placed = (P("ctx", None), P("ctx", None), P("ctx", None), P("ctx", None), P(), P("ctx", None))
    return jax.shard_map(
        shards, mesh=mesh, in_specs=placed, out_specs=P("ctx", None), check_vma=False
    )
```

```python
import functools
import jax
import jax.numpy as jnp
from jax import lax
from jax.experimental import pallas as pl
from jax.experimental.pallas import tpu as pltpu
from jax.sharding import PartitionSpec as P

HEAD = 128
CHUNK = 256
GROUPS = 4
EPSILON = 1e-06
F32 = jnp.float32
BF16 = jnp.bfloat16
MESH = pl.DeviceIdType.MESH


def dot(a, b, dims=((1,), (0,))):
    return lax.dot_general(a, b, (dims, ((), ())), preferred_element_type=F32)


def other(me, mask):
    bit = 1
    out = me
    while bit <= mask:
        if mask & bit:
            out = out + bit * (1 - 2 * ((me // bit) % 2))
        bit *= 2
    return out


def transfers(levels, columns):
    names = [("first", i, g) for i in range(2) for g in range(GROUPS)]
    for l in range(1, levels):
        names += [(kind, l, g) for kind in ("stage", "pass") for g in range(GROUPS)]
    names += [("up", s) for s in range(2)] + [("down", s) for s in range(2)]
    names += [("z", j, s) for j in range(columns) for s in range(2)]
    names += [(kind, j, s) for kind in ("x", "y") for j in range(columns) for s in range(2)]
    names += [(kind, j) for kind in ("dx", "dy") for j in range(columns) if j != 1]
    names += [("dz", s) for s in range(2)]
    names += [(kind, j) for kind in ("c0", "c2", "c4", "c6") for j in range(columns)]
    return {name: at for at, name in enumerate(names)}


def nth_column(me, k, columns):
    column = me // 8
    if k < 2:
        return column + k * (1 - 2 * (column % 2))
    pair, step, pairs = column // 2, k // 2, columns // 2
    upper = pair // (pairs // 2)
    low = pair + upper * (pairs - 1 - 2 * pair)
    inside = (step <= 2 * low).astype(jnp.int32)
    near = low + (step + 1) // 2 * (1 - 2 * (step % 2))
    found = inside * near + (1 - inside) * step
    found = found + upper * (pairs - 1 - 2 * found)
    above = (found > pair).astype(jnp.int32)
    return 2 * found + above * (k % 2) + (1 - above) * (1 - k % 2)


def plane_rows(me, k, columns, part):
    return pl.ds(pl.multiple_of(nth_column(me, k, columns) * (8 * part), 8 * part), 8 * part)


def splits(part):
    return 4 * part % HEAD == 0


def half_plane_rows(me, k, columns, far, part):
    here = me // 4 % 2
    first = nth_column(me, k, columns) * 2 + (1 - here if far else here)
    return pl.ds(pl.multiple_of(first * (4 * part), 4 * part), 4 * part)


def kernel(n, q_hbm, k_hbm, v_hbm, gate_hbm, gain_hbm, w_hbm, acc, k, whole,
           q, v, gate_ref, gain_ref, turned, gates, gains, prefix, running, buckets, first, sends,
           load_sem, send_sem, recv_sem):
    rows, width = q.shape
    heads, chunks = width // HEAD, rows // CHUNK
    half = heads // 2
    group = half // GROUPS
    levels = n.bit_length() - 1
    columns = n // 8
    top = levels - 1
    part = w_hbm.shape[0]
    ids = transfers(levels, columns)
    me = lax.axis_index("ctx")
    core = me % 2
    column = me // 8
    flags = [(me // (1 << l)) % 2 for l in range(levels)]

    def part_of(core_bit, g):
        return pl.ds(core_bit * half + g * group, group)

    def side_of(i):
        return 1 - core if i == 0 else core

    def load(hbm, buffer, kind, at, i, g):
        sem = load_sem.at[kind, at]
        if kind == 2:
            rows_here = pl.ds(at * CHUNK, CHUNK)
            return pltpu.make_async_copy(hbm.at[rows_here], buffer.at[rows_here], sem)
        if kind == 3:
            return pltpu.make_async_copy(hbm, buffer, sem)
        wide = group * HEAD
        cols = pl.ds(pl.multiple_of(side_of(i) * (half * HEAD) + g * wide, wide), wide)
        return pltpu.make_async_copy(hbm.at[:, cols], buffer.at[:, cols], sem)

    def loads(i, g):
        at = g * 2 + i
        return load(k_hbm, k, 0, at, i, g), load(v_hbm, v, 1, at, i, g)

    has_up = column < columns - 1
    has_down = column > 0
    barrier = pltpu.get_barrier_semaphore()

    def greet(device):
        pl.semaphore_signal(barrier, inc=1, device_id=(device,), device_id_type=MESH)

    for mask in (1, 2, 4):
        greet(other(me, mask))
    pl.when(has_up)(lambda: greet(me + 8))
    pl.when(has_down)(lambda: greet(me - 8))

    for g in range(GROUPS):
        for i in range(2):
            for one in loads(i, g):
                one.start()
    gate_load = load(gate_hbm, gate_ref, 3, 1, 0, 0)
    gain_load = load(gain_hbm, gain_ref, 3, 2, 0, 0)
    gate_load.start()
    gain_load.start()
    q_loads = [load(q_hbm, q, 2, c, 0, 0) for c in range(chunks)]
    for one in q_loads:
        one.start()

    inside = has_up.astype(jnp.int32) + has_down.astype(jnp.int32)
    pl.semaphore_wait(barrier, 3 + inside)

    def z_sem(at, s):
        return ids["z", 0, 0] + 2 * at + s

    def copy(name, src, dst, device, landing=None):
        at = ids[name]
        landing = at if landing is None else landing
        return pltpu.make_async_remote_copy(
            src_ref=src, dst_ref=dst, send_sem=send_sem.at[at], recv_sem=recv_sem.at[landing],
            device_id=(device,), device_id_type=MESH,
        )

    side_width = whole.shape[1] // 2

    place_of = [nth_column(me, k, columns) for k in range(columns)]

    def block(device, side=None):
        at = pl.ds(pl.multiple_of(device * part, part), part)
        if side is None:
            return whole.at[at]
        return whole.at[at, pl.ds(side * side_width, side_width)]

    def shard(mask, k, side=None):
        return block(other(me, mask) + (place_of[k] - column) * 8, side)

    def own(side):
        return w_hbm.at[:, pl.ds(side * side_width, side_width)]

    def place(l):
        return column % (2 << (l - 3))

    def receives(l):
        return flags[l] == 1

    def origin(l):
        return place(l) == (1 << (l - 3)) - 1

    def relays(l):
        return jnp.logical_and(place(l) >= 1 << (l - 3), place(l) < (2 << (l - 3)) - 1)

    def send(name, relay=False):
        kind, j = name[:2]
        if kind == "first":
            at = part_of(side_of(j), name[2])
            return copy(name, first.at[at], buckets.at[0, at], other(me, 1))
        if kind in ("stage", "pass"):
            g = name[2]
            here = buckets.at[j, part_of(core, g)]
            if kind == "pass":
                return copy(name, here, here, other(me, 1))
            src = here if relay else sends.at[j - 1, pl.ds(g * group, group)]
            return copy(name, src, here, other(me, 1 << j) if j < 3 else me + 8)
        if kind == "dz":
            return copy(name, shard(6, 0, j), shard(6, 0, j), other(me, 8))
        if kind in ("up", "down"):
            return copy(name, own(j), shard(0, 0, j), me + 8 if kind == "up" else me - 8, z_sem(column, j))
        if kind == "z":
            s = name[2]
            at = shard(0, j, s)
            onward = 1 - 2 * (place_of[j] > column).astype(jnp.int32)
            return copy(name, at, at, me + 8 * onward, z_sem(place_of[j], s))
        if kind in ("x", "y"):
            s = name[2]
            src = own(s) if j == 0 else shard(0, j, s)
            return copy(name, src, shard(0, j, s), other(me, {"x": 2, "y": 4}[kind]))
        if kind == "dy":
            return copy(name, shard(2, j, 0), shard(2, j, 0), other(me, 4))
        if kind == "dx":
            return copy(name, shard(4, j, 1), shard(4, j, 1), other(me, 2))
        mask = int(kind[1])
        src = w_hbm if mask == 0 and j == 0 else shard(mask, j)
        return copy(name, src, shard(mask, j), other(me, 1))

    def arrival(name):
        kind, j = name[:2]
        if kind == "first":
            dst = buckets.at[0, part_of(side_of(1 - j), name[2])]
        elif kind == "stage":
            dst = buckets.at[j, part_of(core, name[2])]
        elif kind == "pass":
            dst = buckets.at[j, part_of(1 - core, name[2])]
        elif kind == "dz":
            dst = shard(6, 1, j)
        elif kind == "z":
            dst = shard(0, j, name[2])
            return copy(name, dst, dst, other(me, 1), z_sem(place_of[j], name[2]))
        elif kind in ("x", "y"):
            dst = shard({"x": 2, "y": 4}[kind], j, name[2])
        elif kind == "dy":
            dst = shard(6, j, 0)
        elif kind == "dx":
            dst = shard(6, j, 1)
        else:
            dst = shard(1 ^ int(kind[1]), j)
        return copy(name, dst, dst, other(me, 1))

    def start(*name):
        send(name).start()

    def receive(*name):
        arrival(name).wait_recv()

    mine = pltpu.make_async_copy(w_hbm, shard(0, 0), load_sem.at[3, 0])
    mine.start()
    start("x", 0, 0)
    start("y", 0, 0)
    pl.when(has_up)(lambda: start("up", 0))
    pl.when(has_down)(lambda: start("down", 0))
    start("y", 0, 1)
    pl.when(has_up)(lambda: start("up", 1))
    pl.when(has_down)(lambda: start("down", 1))
    start("c0", 0)

    for l in range(3, levels):
        @pl.when(flags[l] == 0)
        def _(l=l):
            buckets[l] = jnp.zeros(buckets.shape[1:], BF16)

    def states(i, g):
        for one in loads(i, g):
            one.wait()
        for e in range(group):
            h = side_of(i) * half + g * group + e
            cols = pl.ds(pl.multiple_of(h * HEAD, HEAD), HEAD)
            sofar = jnp.zeros((HEAD, HEAD), F32)
            for c in range(chunks):
                at = slice(c * CHUNK, (c + 1) * CHUNK)
                prefix[c, h] = sofar.astype(BF16)
                flipped = v[at, cols].T
                turned[cols, at] = flipped
                sofar = sofar + dot(flipped, k[at, cols])
            first[h] = sofar.astype(BF16)
            if i == 1:
                running[g * group + e] = sofar
        start("first", i, g)

    def send_on(l, g):
        at = pl.ds(g * group, group)

        def go():
            sends[l, at] = running[at].astype(BF16)
            start("stage", l + 1, g)

        if l + 1 < 3:
            go()
        else:
            pl.when(origin(l + 1))(go)

    def advance_first(g):
        receive("first", 0, g)
        at = pl.ds(g * group, group)
        running[at] = running[at] + buckets[0, part_of(core, g)].astype(F32)
        send_on(0, g)

    def advance(l, g):
        def arrived():
            receive("stage", l, g)
            if l >= 3:
                @pl.when(relays(l))
                def _():
                    send(("stage", l, g), relay=True).start()
            if l + 1 < levels:
                at = pl.ds(g * group, group)
                running[at] = running[at] + buckets[l, part_of(core, g)].astype(F32)

        def passing():
            start("pass", l, g)

        if l < 3:
            arrived()
        else:
            pl.when(receives(l))(arrived)
        if l + 1 < levels:
            send_on(l, g)
        if l < 3:
            passing()
        else:
            pl.when(receives(l))(passing)

    def passed(l, g):
        if l < 3:
            receive("pass", l, g)
        else:
            pl.when(receives(l))(lambda: receive("pass", l, g))

    def forwards(k):
        down = place_of[k] > column
        return jnp.logical_or(jnp.logical_and(down, has_down), jnp.logical_and(jnp.logical_not(down), has_up))

    def z_forward(k, s):
        pl.when(forwards(k))(lambda: start("z", k, s))

    def z_arrived(k, s):
        receive("z", k, s)

    def sides_arrived(j):
        for s in range(2):
            receive("x", j, s)
            receive("y", j, s)
        start("c2", j)
        start("c4", j)

    def diagonals(j):
        start("dy", j)
        start("dx", j)

    def diagonal_arrived(j):
        if j == 1:
            for s in range(2):
                receive("dz", s)
        else:
            receive("dy", j)
            receive("dx", j)
        start("c6", j)

    def heads_of(g):
        return [side * half + g * group + e for side in range(2) for e in range(group)]

    def body(function, g, tasks):
        for c in range(chunks):
            function(g, c, slice(c * CHUNK, (c + 1) * CHUNK))
            if c in tasks:
                tasks[c]()

    def weight(l, h, at):
        row = (l + 1) * heads + h
        return gates[row : row + 1, at]

    def spot(h, c):
        down, across = divmod(h * chunks, heads // 2)
        return slice(down * HEAD, (down + 1) * HEAD), slice((across + c) * CHUNK, (across + c + 1) * CHUNK)

    def local(g, c, at):
        causal = lax.broadcasted_iota(jnp.int32, (CHUNK, CHUNK), 0) <= lax.broadcasted_iota(
            jnp.int32, (CHUNK, CHUNK), 1
        )
        for h in heads_of(g):
            cols = slice(h * HEAD, (h + 1) * HEAD)
            stack = jnp.concatenate([k[at, cols], prefix[c, h], buckets[0, h]], axis=0)
            product = dot(stack, q[at, cols], ((1,), (1,)))
            scores = jnp.where(causal, product[:CHUNK], 0.0).astype(BF16)
            mixed = dot(turned[cols, at], scores) + product[CHUNK : CHUNK + HEAD]
            acc[spot(h, c)] = mixed * weight(-1, h, at) + product[CHUNK + HEAD :] * weight(0, h, at)

    def add_levels(c, at, h, wanted):
        cols = slice(h * HEAD, (h + 1) * HEAD)
        stack = jnp.concatenate([buckets[l, h] for l in wanted], axis=0)
        product = dot(stack, q[at, cols], ((1,), (1,)))
        sofar = acc[spot(h, c)]
        for i, l in enumerate(wanted):
            sofar = sofar + weight(l, h, at) * product[i * HEAD : (i + 1) * HEAD]
        return sofar

    def middle(g, c, at):
        for h in heads_of(g):
            acc[spot(h, c)] = add_levels(c, at, h, range(1, top - 1))

    def last(g, c, at):
        for h in heads_of(g):
            cols = slice(h * HEAD, (h + 1) * HEAD)
            attended = add_levels(c, at, h, range(top - 1, levels))
            squares = jnp.mean(attended * attended, axis=0, keepdims=True)
            gain = jnp.concatenate([gains[cols, :]] * (CHUNK // HEAD), axis=1)
            normed = attended * lax.rsqrt(squares + EPSILON) * gain
            k[at, cols] = normed.astype(BF16).T

    def z1_arrived(s):
        z_arrived(1, s)
        z_forward(1, s)

        @pl.when(forwards(2))
        def _():
            z_arrived(2, s)
            z_forward(2, s)

        start("x", 1, s)
        if s == 1:
            start("c0", 1)

    def z2_arrived(s):
        pl.when(jnp.logical_not(forwards(2)))(lambda: z_arrived(2, s))
        if s == 0:
            start("x", 2, 0)
            start("y", 2, 0)
        else:
            sides_arrived(0)
            diagonals(0)
            start("x", 2, 1)
            start("y", 2, 1)
            start("c0", 2)

    late = relays(top)

    def forward_3(s):
        def go():
            z_arrived(3, s)
            z_forward(3, s)

        return go

    def forward_3_early():
        for s in range(2):
            pl.when(jnp.logical_and(forwards(3), jnp.logical_not(late)))(forward_3(s))

    def forward_3_late(s):
        pl.when(jnp.logical_and(forwards(3), late))(forward_3(s))

    def z3_arrived(s):
        pl.when(jnp.logical_not(forwards(3)))(lambda: z_arrived(3, s))
        start("x", 3, s)
        start("y", 3, s)
        if s == 1:
            start("c0", 3)

    def last_of_first():
        advance(1, 3)
        for s in range(2):
            start("y", 1, s)

    def all_diagonal_0():
        diagonal_arrived(0)
        for s in range(2):
            start("dz", s)

    def all_sides_2():
        sides_arrived(2)
        diagonals(2)

    def passed_middle(g):
        for l in range(1, top - 1):
            passed(l, g)

    def passed_last(g):
        passed(top - 1, g)
        passed(top, g)

    for g in range(GROUPS):
        states(0, g)
        if g:
            advance_first(g - 1)
        states(1, g)
    advance_first(GROUPS - 1)
    start("x", 0, 1)
    gate_load.wait()
    gain_load.wait()
    for b in range(rows // HEAD):
        at = slice(b * HEAD, (b + 1) * HEAD)
        tile = gate_ref[at, :].astype(F32).T
        scale = [jnp.ones((heads, HEAD), F32)] + [
            jnp.full((heads, HEAD), flags[l].astype(F32)) for l in range(levels)
        ]
        rest = tile.shape[0] - heads * len(scale)
        if rest:
            scale.append(jnp.zeros((rest, HEAD), F32))
        gates[:, at] = tile * jnp.concatenate(scale, axis=0)
    for h in range(heads):
        cols = slice(h * HEAD, (h + 1) * HEAD)
        gains[cols, :] = jnp.broadcast_to(gain_ref[:, cols], (HEAD, HEAD)).T

    for g in range(GROUPS):
        receive("first", 1, g)
    for one in q_loads:
        one.wait()
    body(local, 0, {1: lambda: z1_arrived(0), 3: lambda: advance(1, 0)})
    body(local, 1, {2: lambda: advance(1, 1), 3: lambda: z1_arrived(1)})
    body(local, 2, {1: lambda: advance(1, 2), 3: lambda: advance(2, 0)})
    body(local, 3, {0: last_of_first, 1: lambda: z2_arrived(0), 2: lambda: advance(2, 1)})
    advance(2, 2)
    z2_arrived(1)
    advance(2, 3)
    for l in range(3, top - 1):
        for g in range(GROUPS):
            advance(l, g)
    passed_middle(0)
    body(middle, 0, {})
    forward_3_early()
    advance(top - 1, 0)
    passed_middle(1)
    body(middle, 1, {})
    advance(top - 1, 1)
    passed_middle(2)
    body(middle, 2, {})
    advance(top - 1, 2)
    passed_middle(3)
    body(middle, 3, {})
    advance(top - 1, 3)
    advance(top, 0)
    advance(top, 1)
    passed_last(0)
    body(last, 0, {2: lambda: advance(top, 2)})
    advance(top, 3)
    forward_3_late(0)
    forward_3_late(1)
    passed_last(1)
    body(last, 1, {3: lambda: sides_arrived(1)})
    passed_last(2)
    body(last, 2, {1: lambda: z3_arrived(0), 3: all_diagonal_0})
    passed_last(3)
    body(last, 3, {})

    def rest_columns():
        for j in range(4, columns):
            for s in range(2):
                z_arrived(j, s)
                z_forward(j, s)
                start("x", j, s)
                start("y", j, s)
            start("c0", j)
        for j in range(4, columns):
            sides_arrived(j)
            diagonals(j)
        for j in range(4, columns):
            diagonal_arrived(j)

    def project(pieces, fresh, tasks):
        wide = whole.shape[1] // chunks

        def step(c, carry):
            cols = pl.ds(pl.multiple_of(c * wide, wide), wide)
            product = None
            for planes in pieces:
                more = dot(k[:, planes], whole[planes, cols])
                product = more if product is None else product + more
            acc[:, cols] = product if fresh else acc[:, cols] + product
            for point, task in tasks.items():
                pl.when(c == point)(task)
            return carry

        lax.fori_loop(0, chunks, step, 0)

    mine.wait()
    for kind in ("c0", "c2", "c4", "c6"):
        receive(kind, 0)
    for kind in ("c0", "c2"):
        receive(kind, 1)

    def rest_of_3():
        z3_arrived(1)
        all_sides_2()

    def all_sides_3():
        sides_arrived(3)
        diagonals(3)

    apart = splits(part)
    pieces = [plane_rows(me, 0, columns, part)]
    if apart:
        pieces.append(half_plane_rows(me, 1, columns, False, part))
    project(pieces, True, {0: rest_of_3})
    if columns > 4:
        rest_columns()
    for j in range(4, columns):
        for kind in ("c0", "c2", "c4", "c6"):
            receive(kind, j)
        project([plane_rows(me, j, columns, part)], False, {})
    for kind in ("c0", "c2"):
        receive(kind, 2)
    if apart:
        project([half_plane_rows(me, 2, columns, False, part)], False, {3: all_sides_3})
    else:
        all_sides_3()
    diagonal_arrived(1)
    for kind in ("c4", "c6"):
        receive(kind, 1)
    if apart:
        project([half_plane_rows(me, 1, columns, True, part)], False, {3: lambda: diagonal_arrived(2)})
    else:
        project([plane_rows(me, 1, columns, part)], False, {3: lambda: diagonal_arrived(2)})
    for kind in ("c0", "c2"):
        receive(kind, 3)
    if apart:
        project([half_plane_rows(me, 3, columns, False, part)], False, {})
    diagonal_arrived(3)
    for name in ids:
        if name == ("c6", 3):
            continue
        if name[0] == "stage" and name[1] >= 3:
            cond = jnp.logical_or(origin(name[1]), relays(name[1]))
        elif name[0] == "pass" and name[1] >= 3:
            cond = receives(name[1])
        elif name[0] in ("up", "down"):
            cond = has_up if name[0] == "up" else has_down
        elif name[0] == "z":
            if name[1] == 0:
                continue
            cond = forwards(name[1])
        else:
            send(name).wait_send()
            continue
        pl.when(cond)(lambda name=name: send(name).wait_send())
    for j in (2, 3):
        for kind in ("c4", "c6"):
            receive(kind, j)
    send(("c6", 3)).wait_send()


def project_kernel(n, part, acc_ref, normed_ref, whole_ref, out_ref):
    step = out_ref.shape[0]
    at = pl.ds(pl.multiple_of(pl.program_id(0) * step, step), step)
    me = lax.axis_index("ctx")
    product = acc_ref[at, :]
    for j in (2, 3):
        planes = half_plane_rows(me, j, n // 8, True, part) if splits(part) else plane_rows(me, j, n // 8, part)
        product = product + dot(normed_ref[at, planes], whole_ref[planes, :])
    out_ref[...] = product.astype(BF16)


def shards(queries, keys, values, level_gate, norm_gain, out_weight):
    n = lax.axis_size("ctx")
    rows, width = queries.shape
    heads, chunks = width // HEAD, rows // CHUNK
    levels = n.bit_length() - 1
    count = len(transfers(levels, n // 8))
    vmem = pl.BlockSpec(memory_space=pltpu.VMEM)
    hbm = pl.BlockSpec(memory_space=pltpu.HBM)
    out_width = out_weight.shape[1]
    weight_rows = n * out_weight.shape[0]
    acc, normed, whole = pl.pallas_call(
        functools.partial(kernel, n),
        out_shape=[
            pltpu.VMEM((rows, width), F32),
            pltpu.VMEM((rows, width), BF16),
            pltpu.VMEM((weight_rows, out_width), BF16),
        ],
        in_specs=[hbm] * 6,
        out_specs=[vmem] * 3,
        scratch_shapes=[
            pltpu.VMEM((rows, width), BF16),
            pltpu.VMEM((rows, width), BF16),
            pltpu.VMEM(level_gate.shape, BF16),
            pltpu.VMEM((1, width), F32),
            pltpu.VMEM((width, rows), BF16),
            pltpu.VMEM((level_gate.shape[1], rows), F32),
            pltpu.VMEM((width, HEAD), F32),
            pltpu.VMEM((chunks, heads, HEAD, HEAD), BF16),
            pltpu.VMEM((heads // 2, HEAD, HEAD), F32),
            pltpu.VMEM((levels, heads, HEAD, HEAD), BF16),
            pltpu.VMEM((heads, HEAD, HEAD), BF16),
            pltpu.VMEM((levels - 1, heads // 2, HEAD, HEAD), BF16),
            pltpu.SemaphoreType.DMA((4, max(2 * GROUPS, chunks))),
            pltpu.SemaphoreType.DMA((count,)),
            pltpu.SemaphoreType.DMA((count,)),
        ],
        compiler_params=pltpu.CompilerParams(
            collective_id=0, has_side_effects=True, vmem_limit_bytes=40 * 1024 * 1024
        ),
        name="layer",
    )(queries, keys, values, level_gate, norm_gain.reshape(1, -1), out_weight)
    step = rows // 2
    return pl.pallas_call(
        functools.partial(project_kernel, n, out_weight.shape[0]),
        grid=(rows // step,),
        out_shape=jax.ShapeDtypeStruct((rows, out_width), BF16),
        in_specs=[vmem] * 3,
        out_specs=pl.BlockSpec((step, out_width), lambda i: (i, 0)),
        compiler_params=pltpu.CompilerParams(vmem_limit_bytes=16 * 1024 * 1024),
        name="project",
    )(acc, normed, whole)


def solution(mesh):
    placed = (P("ctx", None), P("ctx", None), P("ctx", None), P("ctx", None), P(), P("ctx", None))
    return jax.shard_map(
        shards, mesh=mesh, in_specs=placed, out_specs=P("ctx", None), check_vma=False
    )
```
